256 devices in a mesh: row: 16 (over z, core), col: 16 (over y, x).
Axes of the slice: x: 4, y: 4, z: 8, core: 2. Of those that a mesh axis runs over, the one named last changes fastest.
Arguments:
- rhs: float32 [24576, 12288], P('row', 'col'), may hold values from -6 to 6
- panels_l: float32 [4, 24576, 512], P(None, 'row', 'col'), may hold values from -0.25 to 0.25
- diag_inverse: float32 [4, 512, 512], P(None, None, 'col'), may hold values from -1.5 to 1.5, as said below
Outputs:
- solved_rhs: float32 [24576, 12288], P('row', 'col')
The draws below stay inside these ranges and needn't reach their ends.
Inputs may be any that keep to these rules, and one draw needn't show every extreme that they name: `diag_inverse`: each tile is lower triangular with diagonal entries between 0.5 and 1.5.
All inputs are finite; a program needn't handle non-finite values.
Results may differ from the reference program's by a relative error of at most 0.00016.
Values sent between devices are 32-bit elements; how exact they have to be, the bound alone decides.
A program may use at most 128 MiB of HBM per device.

```python
import jax
import jax.numpy as jnp
from jax import lax

PANEL = 512
PANELS = 4
ROWS = 24576
RHS = 12288


def draw_diag_inverse(key, part):
    key_off = jax.random.fold_in(key, 11)
    key_diag = jax.random.fold_in(key, 12)
    reach = 1.7 * PANEL ** (-0.5)
    lower_part = jax.random.uniform(key_off, (PANELS, PANEL, PANEL), jnp.float32, -reach, reach)
    lower_part = jnp.tril(lower_part, -1)
    diag_vals = jax.random.uniform(key_diag, (PANELS, PANEL), jnp.float32, 0.5, 1.5)
    eye_table = jnp.eye(PANEL, dtype=jnp.float32)
    return lower_part + diag_vals[:, :, None] * eye_table[None]


def shard_levels(own_key, dims, shards, least, top_value):
    level = 1.0
    for axis_at, parts in shards:
        heights = jax.random.uniform(jax.random.fold_in(jax.random.fold_in(own_key, 6), axis_at), (parts,), jnp.float32, least / len(shards), top_value / len(shards))
        level = level * jnp.repeat(jnp.exp(heights), dims[axis_at] // parts).reshape((-1,) + (1,) * (len(dims) - 1 - axis_at))
    return level


def normal_values(key, dims, deviation, most, pieces=(), kind=jnp.bfloat16):
    gain = shard_levels(key, dims, pieces, -0.22, 0.18) if pieces else 1.0
    entries = jax.random.normal(key, dims, jnp.float32) * deviation * gain
    return jnp.minimum(jnp.maximum(entries, -most), most).astype(kind)


def setup_inputs(seed: int = 0) -> dict:
    key_list = jax.random.split(jax.random.key(seed), 4)
    return {
        "rhs": normal_values(key_list[0], (ROWS, RHS), 1.0, 6.0, ((0, 16), (1, 16)), jnp.float32),
        "panels_l": normal_values(key_list[1], (PANELS, ROWS, PANEL), PANEL ** -0.5, 0.25, ((1, 16), (2, 16)), jnp.float32),
        "diag_inverse": draw_diag_inverse(jax.random.fold_in(key_list[3], 71), 0),
    }


def reference(rhs, panels_l, diag_inverse):
    work = rhs
    for k in range(PANELS):
        low = k * PANEL
        high = low + PANEL
        solved = jnp.dot(diag_inverse[k], work[low:high], precision=lax.Precision.HIGHEST, preferred_element_type=jnp.float32)
        update = jnp.dot(panels_l[k][high:], solved, precision=lax.Precision.HIGHEST, preferred_element_type=jnp.float32)
        work = jnp.concatenate([work[:low], solved, work[high:] - update], axis=0)
    return work
```

```python
import functools

import jax
import jax.numpy as jnp
from jax import lax
from jax.experimental import pallas as pl
from jax.experimental.pallas import tpu as pltpu
from jax.sharding import PartitionSpec as P

MESH = pl.DeviceIdType.MESH
F32, BF16 = jnp.float32, jnp.bfloat16

UNITS = 12
PIECES = 8
SPOTS = 8
TURNS = 15
S_FIRST, S_HOP, S_NUM, S_DEN = 24, 4, 5, 8


def split(v):
    high = v.astype(BF16)
    return high, (v - high.astype(F32)).astype(BF16)


def kernel(
    rhs, pan, diag, out, share, solved, right3, left3,
    io_sem, take_sem, l_recv, l_send, c_recv, c_send, b_recv, b_send, x_send,
):
    row, col = lax.axis_index("row"), lax.axis_index("col")
    z, core = row // 2, row % 2
    y, x = col // 4, col % 4
    rows = out.shape[0]
    panel = solved.shape[1]
    slab = pan.shape[1]
    half_panel = panel // 2
    piece = half_panel // PIECES
    sibling = row + 1 - 2 * core
    down = (row + 2 - 4 * core + 16) % 16
    up = (row - 2 + 4 * core + 16) % 16
    hops = jnp.where(core == 0, z, (8 - z) % 8)

    def at_plane(dy, dx):
        return (row, ((y + dy + 8) % 4) * 4 + (x + dx + 8) % 4)

    def source(ry, rx):
        return ((y + ry + 8) % 4) * 4 + (x + rx + 8) % 4

    def relative(ry, rx):
        return ((ry + 8) % 4) * 4 + (rx + 8) % 4


    def tile_part(unit, part, ry, rx):
        size = slab if part is None else slab // 2
        start = source(ry, rx) * slab + (slab // 2 if part == 1 else 0)
        return share.at[unit, pl.ds(pl.multiple_of(start, slab // 2), size), :]

    def send(unit, part, src, to, slot):
        ref = tile_part(unit, part, *src)
        pltpu.make_async_remote_copy(
            src_ref=ref, dst_ref=ref,
            send_sem=l_send.at[unit, slot],
            recv_sem=l_recv.at[unit, part or 0, relative(src[0] - to[0], src[1] - to[1])],
            device_id=at_plane(*to), device_id_type=MESH,
        ).start()

    def arrive(unit, part, ry, rx):
        ref = tile_part(unit, part, ry, rx)
        pltpu.make_async_remote_copy(
            src_ref=ref, dst_ref=ref,
            send_sem=l_send.at[unit, 0],
            recv_sem=l_recv.at[unit, part or 0, relative(ry, rx)],
            device_id=at_plane(0, 1), device_id_type=MESH,
        ).wait_recv()

    def stage0(unit):
        for slot, to in enumerate(((0, 1), (0, -1), (1, 0), (-1, 0))):
            send(unit, None, (0, 0), to, slot)

    def stage1(unit, step):
        e = 1 - 2 * (unit % 2)
        if step == 0:
            arrive(unit, None, 0, -e)
            send(unit, 0, (0, -e), (0, e), 4)
            send(unit, 0, (0, -e), (1, 0), 5)
            send(unit, 0, (0, -e), (-1, 0), 6)
        elif step == 1:
            arrive(unit, None, e, 0)
            send(unit, 1, (e, 0), (-e, 0), 7)
            send(unit, 1, (e, 0), (0, 1), 8)
            send(unit, 1, (e, 0), (0, -1), 9)
        elif step == 2:
            arrive(unit, None, 0, e)
            send(unit, 0, (0, e), (1, 0), 10)
            send(unit, 0, (0, e), (-1, 0), 11)
            send(unit, 1, (0, e), (0, -e), 12)
        else:
            arrive(unit, None, -e, 0)
            send(unit, 1, (-e, 0), (0, 1), 13)
            send(unit, 1, (-e, 0), (0, -1), 14)
            send(unit, 0, (-e, 0), (e, 0), 15)

    def stage2(unit, step):
        e = 1 - 2 * (unit % 2)
        if step == 0:
            arrive(unit, 0, 0, 2)
            send(unit, 0, (0, 2), (1, 0), 16)
            send(unit, 0, (0, 2), (-1, 0), 17)
            arrive(unit, 1, 2, 0)
            send(unit, 1, (2, 0), (0, 1), 18)
            send(unit, 1, (2, 0), (0, -1), 19)
        elif step == 1:
            arrive(unit, 0, -e, 1)
            send(unit, 0, (-e, 1), (e, 0), 20)
            arrive(unit, 1, 1, e)
            send(unit, 1, (1, e), (0, -e), 21)
        else:
            arrive(unit, 0, -e, -1)
            send(unit, 0, (-e, -1), (e, 0), 22)
            arrive(unit, 1, -1, e)
            send(unit, 1, (-1, e), (0, -e), 23)

    def stage3(unit):
        e = 1 - 2 * (unit % 2)
        arrive(unit, 0, -e, 2)
        send(unit, 0, (-e, 2), (e, 0), 24)
        arrive(unit, 1, 2, e)
        send(unit, 1, (2, e), (0, -e), 25)

    def final(unit):
        e = 1 - 2 * (unit % 2)
        for ry, rx in ((e, 1), (e, -1), (2, 0), (e, 2), (2, 1), (2, -1), (2, 2)):
            arrive(unit, 0, ry, rx)
        for ry, rx in ((1, -e), (-1, -e), (0, 2), (2, -e), (1, 2), (-1, 2), (2, 2)):
            arrive(unit, 1, ry, rx)

    def drain_shares(count):
        def body(unit, _):
            for slot in range(26):
                ref = tile_part(unit, None if slot < 4 else 0, 0, 0)
                pltpu.make_async_remote_copy(
                    src_ref=ref, dst_ref=ref,
                    send_sem=l_send.at[unit, slot], recv_sem=l_recv.at[unit, 0, 0],
                    device_id=at_plane(0, 1), device_id_type=MESH,
                ).wait_send()
            return 0

        lax.fori_loop(0, count, body, 0)


    def strip(k, which, p):
        start = pl.multiple_of(which * half_panel + p * piece, piece)
        return solved.at[k, pl.ds(start, piece), :]

    def hop(k, which, p, send_sem, recv_sem, to):
        ref = strip(k, which, p)
        return pltpu.make_async_remote_copy(
            src_ref=ref, dst_ref=ref, send_sem=send_sem.at[k, p], recv_sem=recv_sem.at[k, p],
            device_id=(to, col), device_id_type=MESH,
        )

    def relay(j, to_sibling):
        k, p = j // PIECES, j % PIECES
        hop(k, core, p, c_send, c_recv, up).wait_recv()

        @pl.when(hops < 7)
        def _():
            hop(k, core, p, c_send, c_recv, down).start()

        if to_sibling:
            hop(k, core, p, b_send, b_recv, sibling).start()

    def from_sibling(k):
        for p in range(PIECES):
            hop(k, 1 - core, p, b_send, b_recv, sibling).wait_recv()


    def convert(src):
        def body(b, _):
            start = pl.multiple_of(b * 32, 32)
            high, low = split(src[pl.ds(start, 32), :])
            right3[pl.ds(start, 32), :] = high
            right3[pl.ds(pl.multiple_of(panel + start, 32), 32), :] = low
            right3[pl.ds(pl.multiple_of(2 * panel + start, 32), 32), :] = high
            return 0

        lax.fori_loop(0, panel // 32, body, 0)

    def unfold(unit):
        def body(b, _):
            start = pl.multiple_of(b * 128, 128)
            for g in range(panel // 128):
                tile = share[unit, pl.ds(start, 128), g * 128 : (g + 1) * 128].T
                high, low = split(tile)
                to = pl.ds(g * 128, 128)
                left3[to, pl.ds(start, 128)] = high
                left3[to, pl.ds(pl.multiple_of(panel + start, 128), 128)] = high
                left3[to, pl.ds(pl.multiple_of(2 * panel + start, 128), 128)] = low
            return 0

        lax.fori_loop(0, panel // 128, body, 0)

    def product(block, dest):
        cols = pl.ds(pl.multiple_of(block * 256, 256), 256)
        to = pl.ds(pl.multiple_of(dest * panel, panel), panel)
        acc = jnp.dot(left3[...], right3[:, cols], preferred_element_type=F32)
        return cols, to, acc

    def subtract(block, dest):
        cols, to, acc = product(block, dest)
        out[to, cols] = out[to, cols] - acc

    def assign(block, dest, k):
        cols, to, acc = product(block, dest)
        out[to, cols] = acc
        solved[k, :, cols] = acc

    def subtract_all(dest):
        def body(block, _):
            subtract(block, dest)
            return 0

        lax.fori_loop(0, 3, body, 0)

    def assign_all(dest, k):
        def body(block, _):
            assign(block, dest, k)
            return 0

        lax.fori_loop(0, 3, body, 0)

    def out_panel(u):
        return out.at[pl.ds(pl.multiple_of(u * panel, panel), panel), :]


    first, second = row == 0, row == 1

    def loop(first, last, body):
        def turn(i, _):
            body(i)
            return 0

        lax.fori_loop(first, last, turn, 0)

    fetch = pltpu.make_async_copy(rhs, out, io_sem.at[0])
    fetch.start()

    def mine(t):
        return share.at[t, pl.ds(pl.multiple_of(col * slab, slab), slab), :]

    def take_factor(t, k, u):
        columns = pl.ds(pl.multiple_of(u * panel, panel), panel)
        return pltpu.make_async_copy(pan.at[k, :, columns], mine(t), take_sem.at[t])

    def take_inverse(t, k):
        return pltpu.make_async_copy(diag.at[k], mine(t), take_sem.at[t])

    @pl.when(row > 1)
    def _():
        loop(0, UNITS, lambda t: take_factor(t, t // 3, t % 3).start())

    @pl.when(first)
    def _():
        take_inverse(0, 0).start()
        take_factor(1, 0, 1).start()
        take_factor(2, 0, 2).start()
        take_inverse(3, 1).start()
        take_factor(4, 1, 2).start()
        take_inverse(5, 2).start()

    @pl.when(second)
    def _():
        loop(0, 3, lambda t: take_factor(t, t, 0).start())
        take_inverse(3, 3).start()
        loop(4, UNITS, lambda t: take_factor(t, (t - 4) // 2, 1 + t % 2).start())

    barrier = pltpu.get_barrier_semaphore()
    for to in (at_plane(0, 1), at_plane(0, -1), at_plane(1, 0), at_plane(-1, 0), (sibling, col), (up, col), (down, col)):
        pl.semaphore_signal(barrier, inc=1, device_id=to, device_id_type=MESH)

    loop(0, jnp.where(first, 6, UNITS), lambda t: take_inverse(t, 0).wait())
    pl.semaphore_wait(barrier, 7)
    fetch.wait()


    def plane_turn(m, count):
        @pl.when(m + 2 < count)
        def _():
            stage0(m + 2)

        @pl.when(m < count)
        def _():
            for i in range(4):
                stage1(m, i)

        @pl.when(m >= 1)
        def _():
            for i in range(3):
                stage2(m - 1, i)
            stage3(m - 1)

    @pl.when(first)
    def _():
        stage0(0)
        stage0(1)

        def turn(m):
            plane_turn(m, 6)

            @pl.when(m >= 1)
            def _():
                q = m - 1
                final(q)
                k = jnp.where(q < 3, 0, jnp.where(q < 5, 1, 2))
                dest = jnp.where(q < 3, q, jnp.where(q < 4, 1, 2))
                is_solve = (q == 0) | (q == 3) | (q == 5)

                @pl.when(q != 2)
                def _():
                    convert(out_panel(k))

                unfold(q)

                @pl.when(is_solve)
                def _():
                    assign_all(dest, k)
                    for p in range(PIECES):
                        hop(k, 0, p, c_send, c_recv, down).start()
                        hop(k, 1, p, x_send, c_recv, sibling).start()
                        hop(k, 0, p, b_send, b_recv, sibling).start()

                @pl.when(jnp.logical_not(is_solve))
                def _():
                    subtract_all(dest)

        loop(0, 7, turn)
        loop(3 * PIECES, 4 * PIECES, lambda j: relay(j, False))
        drain_shares(6)

        def drain(j):
            k, p = j // PIECES, j % PIECES
            hop(k, 0, p, c_send, c_recv, down).wait_send()

            @pl.when(k < 3)
            def _():
                hop(k, 1, p, x_send, c_recv, sibling).wait_send()
                hop(k, 0, p, b_send, b_recv, sibling).wait_send()

        loop(0, 4 * PIECES, drain)

    @pl.when(second)
    def _():
        loop(0, PIECES, lambda j: relay(j, False))
        from_sibling(0)
        stage0(0)
        stage0(1)

        def turn(m):
            plane_turn(m, UNITS)

            @pl.when(m >= 1)
            def _():
                q = m - 1
                final(q)

                @pl.when((q == 1) | (q == 2))
                def _():
                    loop(q * PIECES, (q + 1) * PIECES, lambda j: relay(j, False))
                    from_sibling(q)

                @pl.when(q == 3)
                def _():
                    convert(out_panel(0))

                @pl.when((q < 3) | ((q >= 4) & (q % 2 == 0)))
                def _():
                    convert(solved.at[jnp.where(q < 3, q, (q - 4) // 2)])

                unfold(q)

                @pl.when(q == 3)
                def _():
                    assign_all(0, 3)
                    for p in range(PIECES):
                        hop(3, 1, p, c_send, c_recv, down).start()
                        hop(3, 0, p, x_send, c_recv, sibling).start()

                @pl.when(q != 3)
                def _():
                    subtract_all(jnp.where(q < 3, 0, 1 + q % 2))

        loop(0, UNITS + 1, turn)
        drain_shares(UNITS)
        loop(0, 4 * PIECES, lambda j: hop(j // PIECES, 1, j % PIECES, c_send, c_recv, down).wait_send())
        loop(0, PIECES, lambda p: hop(3, 0, p, x_send, c_recv, sibling).wait_send())


    @pl.when(row > 1)
    def _():
        farthest = jnp.maximum(hops, 8 - hops)
        lag = (S_FIRST + S_HOP * farthest + 16 + 3) // 4

        def relayed(spot):
            ahead = jnp.maximum(spot - S_FIRST - S_HOP * hops, 0)
            return jnp.minimum(ahead * S_NUM // S_DEN, 4 * PIECES)

        def taken(slot):
            ready = jnp.minimum(slot - lag, jnp.maximum(slot - 4, 0) // 2 - 1)
            return jnp.clip(ready + 1, 0, UNITS)

        stage0(0)
        stage0(1)

        def turn(m):
            for i in range(SPOTS):
                if i == 0:

                    @pl.when(m + 2 < UNITS)
                    def _():
                        stage0(m + 2)

                if i < 4:

                    @pl.when(m < UNITS)
                    def _():
                        stage1(m, i)
                elif i < 7:

                    @pl.when((m >= 1) & (m < UNITS + 1))
                    def _():
                        stage2(m - 1, i - 4)
                else:

                    @pl.when((m >= 2) & (m < UNITS + 2))
                    def _():
                        stage3(m - 2)

                spot = m * SPOTS + i
                loop(relayed(spot - 1), relayed(spot), lambda j: relay(j, True))

                slot = 2 * m + i // 4
                q = taken(slot) - 1
                fresh = q >= taken(slot - 1)
                part = i % 4
                if part == 0:

                    @pl.when(fresh)
                    def _():
                        final(q)

                        @pl.when(q % 3 == 0)
                        def _():
                            from_sibling(q // 3)
                            convert(solved.at[q // 3])

                        unfold(q)
                else:

                    @pl.when(fresh)
                    def _():
                        subtract(part - 1, q % 3)

        loop(0, TURNS, turn)
        drain_shares(UNITS)

        def drain(j):
            k, p = j // PIECES, j % PIECES

            @pl.when(hops < 7)
            def _():
                hop(k, core, p, c_send, c_recv, down).wait_send()

            hop(k, core, p, b_send, b_recv, sibling).wait_send()

        loop(0, 4 * PIECES, drain)


def per_device(rhs, panels_l, diag_inverse):
    rows, width = rhs.shape
    count, panel, _ = diag_inverse.shape
    sem = pltpu.SemaphoreType.DMA
    return pl.pallas_call(
        kernel,
        out_shape=jax.ShapeDtypeStruct((rows, width), F32),
        in_specs=[pl.BlockSpec(memory_space=pl.ANY)] * 3,
        out_specs=pl.BlockSpec(memory_space=pltpu.VMEM),
        scratch_shapes=[
            pltpu.VMEM((UNITS, panel, panel), F32),
            pltpu.VMEM((count, panel, width), F32),
            pltpu.VMEM((3 * panel, width), BF16),
            pltpu.VMEM((panel, 3 * panel), BF16),
            sem((1,)),
            sem((UNITS,)),
            sem((UNITS, 2, 16)),
            sem((UNITS, 26)),
            sem((count, PIECES)),
            sem((count, PIECES)),
            sem((count, PIECES)),
            sem((count, PIECES)),
            sem((count, PIECES)),
        ],
        compiler_params=pltpu.CompilerParams(
            collective_id=0, has_side_effects=True, vmem_limit_bytes=60 * 1024 * 1024
        ),
        name="forward_substitution",
    )(rhs, jnp.swapaxes(panels_l, 1, 2), jnp.swapaxes(diag_inverse, 1, 2))


def solution(mesh):
    in_specs = (P("row", "col"), P(None, "row", "col"), P(None, None, "col"))
    out_specs = P("row", "col")
    return jax.shard_map(
        per_device, mesh=mesh, in_specs=in_specs, out_specs=out_specs, check_vma=False
    )
```

```python
import functools

import jax
import jax.numpy as jnp
from jax import lax
from jax.experimental import pallas as pl
from jax.experimental.pallas import tpu as pltpu
from jax.sharding import PartitionSpec as P

MESH = pl.DeviceIdType.MESH
F32, BF16 = jnp.float32, jnp.bfloat16

UNITS = 12
PIECES = 16
GROUP = 4
SPOTS = 8
S_FIRST, S_HOP, S_NUM, S_DEN = 24, 4, 5, 4
GO = 3
LAG = -(-(S_FIRST + 7 * S_HOP + 16) // 4)
SLACK = 11
TURNS = -(-max(UNITS + LAG, 2 * UNITS - 1 + SLACK) // 4)


def split(v):
    high = v.astype(BF16)
    return high, (v - high.astype(F32)).astype(BF16)


def kernel(
    rhs, pan, diag, out, share, solved, right3, left3,
    go_sem, io_sem, take_sem, l_recv, l_send, c_recv, c_send, b_recv, b_send, x_send,
):
    row, col = lax.axis_index("row"), lax.axis_index("col")
    z, core = row // 2, row % 2
    y, x = col // 4, col % 4
    rows = out.shape[0]
    panel = solved.shape[1]
    slab = pan.shape[1]
    half_slab, half_panel = slab // 2, panel // 2
    piece = half_panel // PIECES
    sibling = row + 1 - 2 * core
    down = (row + 2 - 4 * core + 16) % 16
    up = (row - 2 + 4 * core + 16) % 16
    hops = jnp.where(core == 0, z, (8 - z) % 8)

    ys = [lax.rem(y + d, 4) for d in range(4)]
    xs = [lax.rem(x + d, 4) for d in range(4)]
    sources = [[4 * ys[ry] + xs[rx] for rx in range(4)] for ry in range(4)]
    starts = [[slab * v for v in line] for line in sources]

    def at_plane(dy, dx):
        return (row, sources[dy % 4][dx % 4])

    def relative(ry, rx):
        return (ry % 4) * 4 + rx % 4


    def tile_part(unit, part, ry, rx):
        start = starts[ry % 4][rx % 4] + (half_slab if part == 1 else 0)
        size = slab if part is None else half_slab
        return share.at[unit, pl.ds(pl.multiple_of(start, half_slab), size), :]

    def send(unit, part, src, to, slot):
        ref = tile_part(unit, part, *src)
        pltpu.make_async_remote_copy(
            src_ref=ref, dst_ref=ref,
            send_sem=l_send.at[unit, slot],
            recv_sem=l_recv.at[unit, part or 0, relative(src[0] - to[0], src[1] - to[1])],
            device_id=at_plane(*to), device_id_type=MESH,
        ).start()

    def arrive(unit, part, ry, rx):
        ref = tile_part(unit, part, ry, rx)
        pltpu.make_async_remote_copy(
            src_ref=ref, dst_ref=ref,
            send_sem=l_send.at[unit, 0],
            recv_sem=l_recv.at[unit, part or 0, relative(ry, rx)],
            device_id=at_plane(0, 1), device_id_type=MESH,
        ).wait_recv()

    def stage0(unit):
        for slot, to in enumerate(((0, 1), (0, -1), (1, 0), (-1, 0))):
            send(unit, None, (0, 0), to, slot)

    def stage1(unit, e, step):
        if step == 0:
            arrive(unit, None, 0, -e)
            send(unit, 0, (0, -e), (0, e), 4)
            send(unit, 0, (0, -e), (1, 0), 5)
            send(unit, 0, (0, -e), (-1, 0), 6)
        elif step == 1:
            arrive(unit, None, e, 0)
            send(unit, 1, (e, 0), (-e, 0), 7)
            send(unit, 1, (e, 0), (0, 1), 8)
            send(unit, 1, (e, 0), (0, -1), 9)
        elif step == 2:
            arrive(unit, None, 0, e)
            send(unit, 0, (0, e), (1, 0), 10)
            send(unit, 0, (0, e), (-1, 0), 11)
            send(unit, 1, (0, e), (0, -e), 12)
        else:
            arrive(unit, None, -e, 0)
            send(unit, 1, (-e, 0), (0, 1), 13)
            send(unit, 1, (-e, 0), (0, -1), 14)
            send(unit, 0, (-e, 0), (e, 0), 15)

    def stage2(unit, e, step):
        if step == 0:
            arrive(unit, 0, 0, 2)
            send(unit, 0, (0, 2), (1, 0), 16)
            send(unit, 0, (0, 2), (-1, 0), 17)
            arrive(unit, 1, 2, 0)
            send(unit, 1, (2, 0), (0, 1), 18)
            send(unit, 1, (2, 0), (0, -1), 19)
        elif step == 1:
            arrive(unit, 0, -e, 1)
            send(unit, 0, (-e, 1), (e, 0), 20)
            arrive(unit, 1, 1, e)
            send(unit, 1, (1, e), (0, -e), 21)
        else:
            arrive(unit, 0, -e, -1)
            send(unit, 0, (-e, -1), (e, 0), 22)
            arrive(unit, 1, -1, e)
            send(unit, 1, (-1, e), (0, -e), 23)

    def stage3(unit, e):
        arrive(unit, 0, -e, 2)
        send(unit, 0, (-e, 2), (e, 0), 24)
        arrive(unit, 1, 2, e)
        send(unit, 1, (2, e), (0, -e), 25)

    def final(unit):
        def rest(e):
            for ry, rx in ((e, 1), (e, -1), (2, 0), (e, 2), (2, 1), (2, -1), (2, 2)):
                arrive(unit, 0, ry, rx)
            for ry, rx in ((1, -e), (-1, -e), (0, 2), (2, -e), (1, 2), (-1, 2), (2, 2)):
                arrive(unit, 1, ry, rx)

        even = lax.rem(unit, 2) == 0
        pl.when(even)(lambda: rest(1))
        pl.when(jnp.logical_not(even))(lambda: rest(-1))

    def drain_shares(count):
        def body(unit, _):
            for slot in range(26):
                ref = tile_part(unit, None if slot < 4 else 0, 0, 0)
                pltpu.make_async_remote_copy(
                    src_ref=ref, dst_ref=ref,
                    send_sem=l_send.at[unit, slot], recv_sem=l_recv.at[unit, 0, 0],
                    device_id=at_plane(0, 1), device_id_type=MESH,
                ).wait_send()
            return 0

        lax.fori_loop(0, count, body, 0)


    def strip(k, which, p):
        start = pl.multiple_of(which * half_panel + p * piece, piece)
        return solved.at[k, pl.ds(start, piece), :]

    def hop(k, which, p, send_sem, recv_sem, to):
        ref = strip(k, which, p)
        return pltpu.make_async_remote_copy(
            src_ref=ref, dst_ref=ref, send_sem=send_sem.at[k, p], recv_sem=recv_sem.at[k, p],
            device_id=(to, col), device_id_type=MESH,
        )

    def relay(j, to_sibling):
        k, p = lax.div(j, PIECES), lax.rem(j, PIECES)
        hop(k, core, p, c_send, c_recv, up).wait_recv()

        @pl.when(hops < 7)
        def _():
            hop(k, core, p, c_send, c_recv, down).start()

        if to_sibling:

            @pl.when(lax.rem(p, GROUP) == GROUP - 1)
            def _():
                beside(k, core, lax.div(p, GROUP)).start()

    def beside(k, which, g):
        rows = GROUP * piece
        ref = solved.at[k, pl.ds(pl.multiple_of(which * half_panel + g * rows, rows), rows), :]
        return pltpu.make_async_remote_copy(
            src_ref=ref, dst_ref=ref, send_sem=b_send.at[k, g], recv_sem=b_recv.at[k, g],
            device_id=(sibling, col), device_id_type=MESH,
        )

    def from_sibling(k):
        for g in range(PIECES // GROUP):
            beside(k, 1 - core, g).wait_recv()


    def convert(src):
        def body(b, _):
            start = pl.multiple_of(b * 32, 32)
            high, low = split(src[pl.ds(start, 32), :])
            right3[pl.ds(start, 32), :] = high
            right3[pl.ds(pl.multiple_of(panel + start, 32), 32), :] = low
            right3[pl.ds(pl.multiple_of(2 * panel + start, 32), 32), :] = high
            return 0

        lax.fori_loop(0, panel // 32, body, 0)

    def unfold(unit):
        def body(b, _):
            start = pl.multiple_of(b * 128, 128)
            for g in range(panel // 128):
                tile = share[unit, pl.ds(start, 128), g * 128 : (g + 1) * 128].T
                high, low = split(tile)
                to = pl.ds(g * 128, 128)
                left3[to, pl.ds(start, 128)] = high
                left3[to, pl.ds(pl.multiple_of(panel + start, 128), 128)] = high
                left3[to, pl.ds(pl.multiple_of(2 * panel + start, 128), 128)] = low
            return 0

        lax.fori_loop(0, panel // 128, body, 0)

    def product(block, dest):
        cols = pl.ds(pl.multiple_of(block * 256, 256), 256)
        to = pl.ds(pl.multiple_of(dest * panel, panel), panel)
        acc = jnp.dot(left3[...], right3[:, cols], preferred_element_type=F32)
        return cols, to, acc

    def subtract(block, dest):
        cols, to, acc = product(block, dest)
        out[to, cols] = out[to, cols] - acc

    def assign(block, dest, k):
        cols, to, acc = product(block, dest)
        out[to, cols] = acc
        solved[k, :, cols] = acc

    def subtract_all(dest):
        def body(block, _):
            subtract(block, dest)
            return 0

        lax.fori_loop(0, 3, body, 0)

    def assign_all(dest, k):
        def body(block, _):
            assign(block, dest, k)
            return 0

        lax.fori_loop(0, 3, body, 0)

    def out_panel(u):
        return out.at[pl.ds(pl.multiple_of(u * panel, panel), panel), :]


    first, second = row == 0, row == 1

    def loop(first, last, body):
        def turn(i, _):
            body(i)
            return 0

        lax.fori_loop(first, last, turn, 0)

    fetch = pltpu.make_async_copy(rhs, out, io_sem.at[0])
    fetch.start()

    def mine(t):
        return share.at[t, pl.ds(pl.multiple_of(col * slab, slab), slab), :]

    def take_factor(t, k, u):
        columns = pl.ds(pl.multiple_of(u * panel, panel), panel)
        return pltpu.make_async_copy(pan.at[k, :, columns], mine(t), take_sem.at[t])

    def take_inverse(t, k):
        return pltpu.make_async_copy(diag.at[k], mine(t), take_sem.at[t])

    @pl.when(row > 1)
    def _():
        loop(0, UNITS, lambda t: take_factor(t, t // 3, t % 3).start())

    @pl.when(first)
    def _():
        take_inverse(0, 0).start()
        take_factor(1, 0, 1).start()
        take_factor(2, 0, 2).start()
        take_inverse(3, 1).start()
        take_factor(4, 1, 2).start()
        take_inverse(5, 2).start()

    @pl.when(second)
    def _():
        loop(0, 3, lambda t: take_factor(t, t, 0).start())
        take_inverse(3, 3).start()
        loop(4, UNITS, lambda t: take_factor(t, (t - 4) // 2, 1 + t % 2).start())

    barrier = pltpu.get_barrier_semaphore()
    for to in (at_plane(0, 1), at_plane(0, -1), at_plane(1, 0), at_plane(-1, 0), (sibling, col), (up, col), (down, col)):
        pl.semaphore_signal(barrier, inc=1, device_id=to, device_id_type=MESH)

    loop(0, jnp.where(first, 6, UNITS), lambda t: take_inverse(t, 0).wait())
    pl.semaphore_wait(barrier, 7)


    def plane_turn(m, first_unit, last_unit):
        @pl.when(m + 2 < last_unit)
        def _():
            stage0(m + 2)

        def relays(e):
            @pl.when(m < last_unit)
            def _():
                for i in range(4):
                    stage1(m, e, i)

            @pl.when((m >= first_unit + 1) & (m < last_unit + 1))
            def _():
                for i in range(3):
                    stage2(m - 1, -e, i)

            @pl.when((m >= first_unit + 2) & (m < last_unit + 2))
            def _():
                stage3(m - 2, e)

        even = lax.rem(m, 2) == 0
        pl.when(even)(lambda: relays(1))
        pl.when(jnp.logical_not(even))(lambda: relays(-1))

    @pl.when(first)
    def _():
        stage0(0)
        stage0(1)

        def turn(m):
            @pl.when(m == GO)
            def _():
                pl.semaphore_signal(go_sem, inc=1, device_id=(sibling, col), device_id_type=MESH)

            plane_turn(m, 0, 6)

            @pl.when(m == 3)
            def _():
                fetch.wait()

            @pl.when(m >= 3)
            def _():
                q = m - 3
                final(q)
                k = jnp.where(q < 3, 0, jnp.where(q < 5, 1, 2))
                dest = jnp.where(q < 3, q, jnp.where(q < 4, 1, 2))
                is_solve = (q == 0) | (q == 3) | (q == 5)

                @pl.when(q != 2)
                def _():
                    convert(out_panel(k))

                unfold(q)

                @pl.when(is_solve)
                def _():
                    assign_all(dest, k)
                    for p in range(PIECES):
                        hop(k, 0, p, c_send, c_recv, down).start()
                        hop(k, 1, p, x_send, c_recv, sibling).start()
                    for g in range(PIECES // GROUP):
                        beside(k, 0, g).start()

                @pl.when(jnp.logical_not(is_solve))
                def _():
                    subtract_all(dest)

        loop(0, 9, turn)
        loop(3 * PIECES, 4 * PIECES, lambda j: relay(j, False))
        drain_shares(6)

        def drain(j):
            k, p = j // PIECES, j % PIECES
            hop(k, 0, p, c_send, c_recv, down).wait_send()

            @pl.when(k < 3)
            def _():
                hop(k, 1, p, x_send, c_recv, sibling).wait_send()

                @pl.when(lax.rem(p, GROUP) == 0)
                def _():
                    beside(k, 0, lax.div(p, GROUP)).wait_send()

        loop(0, 4 * PIECES, drain)

    @pl.when(second)
    def _():
        pl.semaphore_wait(go_sem, 1)
        stage0(0)
        stage0(1)

        def early_turn(m):
            plane_turn(m, 0, 4)

            @pl.when(m == 3)
            def _():
                fetch.wait()

            @pl.when(m >= 3)
            def _():
                q = m - 3
                final(q)

                @pl.when(q < 3)
                def _():
                    loop(q * PIECES, (q + 1) * PIECES, lambda j: relay(j, False))
                    from_sibling(q)
                    convert(solved.at[q])

                @pl.when(q == 3)
                def _():
                    convert(out_panel(0))

                unfold(q)

                @pl.when(q == 3)
                def _():
                    assign_all(0, 3)
                    for p in range(PIECES):
                        hop(3, 1, p, c_send, c_recv, down).start()
                        hop(3, 0, p, x_send, c_recv, sibling).start()

                @pl.when(q != 3)
                def _():
                    subtract_all(0)

        loop(0, 7, early_turn)
        stage0(4)
        stage0(5)

        def turn(m):
            plane_turn(m, 4, UNITS)

            @pl.when(m >= 7)
            def _():
                q = m - 3
                final(q)

                @pl.when(q % 2 == 0)
                def _():
                    convert(solved.at[(q - 4) // 2])

                unfold(q)
                subtract_all(1 + q % 2)

        loop(4, UNITS + 3, turn)
        drain_shares(UNITS)
        loop(0, 4 * PIECES, lambda j: hop(j // PIECES, 1, j % PIECES, c_send, c_recv, down).wait_send())
        loop(0, PIECES, lambda p: hop(3, 0, p, x_send, c_recv, sibling).wait_send())


    @pl.when(row > 1)
    def _():
        farthest = jnp.maximum(hops, 8 - hops)
        lag = lax.div(S_FIRST + S_HOP * farthest + 16 + 3, 4)
        due = S_FIRST + S_HOP * hops

        def relayed(spot):
            ahead = jnp.maximum(spot - due, 0)
            return jnp.minimum(lax.div(ahead * S_NUM, S_DEN), 4 * PIECES)

        def taken(slot):
            ready = jnp.minimum(slot - lag + 1, lax.div(jnp.maximum(slot - SLACK + 2, 0), 2))
            return jnp.clip(ready, 0, UNITS)

        stage0(0)
        stage0(1)

        def tile_turn(m, e, carry):
            before, done = carry
            for i in range(SPOTS):
                if i == 0:

                    @pl.when(m + 2 < UNITS)
                    def _():
                        stage0(m + 2)

                if i % 2 == 0:

                    @pl.when(m < UNITS)
                    def _():
                        stage1(m, e, i // 2)
                elif i < 7:

                    @pl.when((m >= 2) & (m < UNITS + 2))
                    def _():
                        stage2(m - 2, e, i // 2)
                else:

                    @pl.when((m >= 3) & (m < UNITS + 3))
                    def _():
                        stage3(m - 3, -e)

                now = relayed(m * SPOTS + i)
                loop(done, now, lambda j: relay(j, True))
                done = now

                part = i % 4
                if part == 0:
                    after = taken(2 * m + i // 4)
                    q = after - 1
                    k, u = lax.div(jnp.maximum(q, 0), 3), lax.rem(jnp.maximum(q, 0), 3)
                    fresh = after > before
                    before = after

                    @pl.when(fresh)
                    def _():
                        final(q)

                        @pl.when(q == 0)
                        def _():
                            fetch.wait()

                        @pl.when(u == 0)
                        def _():
                            from_sibling(k)
                            convert(solved.at[k])

                        unfold(q)
                else:

                    @pl.when(fresh)
                    def _():
                        subtract(part - 1, u)

            return before, done

        def turn(t, carry):
            carry = tile_turn(2 * t, 1, carry)
            return tile_turn(2 * t + 1, -1, carry)

        lax.fori_loop(0, TURNS, turn, (jnp.int32(0), jnp.int32(0)))
        drain_shares(UNITS)

        def drain(j):
            k, p = j // PIECES, j % PIECES

            @pl.when(hops < 7)
            def _():
                hop(k, core, p, c_send, c_recv, down).wait_send()

            @pl.when(lax.rem(p, GROUP) == 0)
            def _():
                beside(k, core, lax.div(p, GROUP)).wait_send()

        loop(0, 4 * PIECES, drain)


def per_device(rhs, panels_l, diag_inverse):
    rows, width = rhs.shape
    count, panel, _ = diag_inverse.shape
    sem = pltpu.SemaphoreType.DMA
    return pl.pallas_call(
        kernel,
        out_shape=pltpu.VMEM((rows, width), F32),
        in_specs=[pl.BlockSpec(memory_space=pl.ANY)] * 3,
        out_specs=pl.BlockSpec(memory_space=pltpu.VMEM),
        scratch_shapes=[
            pltpu.VMEM((UNITS, panel, panel), F32),
            pltpu.VMEM((count, panel, width), F32),
            pltpu.VMEM((3 * panel, width), BF16),
            pltpu.VMEM((panel, 3 * panel), BF16),
            pltpu.SemaphoreType.REGULAR,
            sem((1,)),
            sem((UNITS,)),
            sem((UNITS, 2, 16)),
            sem((UNITS, 26)),
            sem((count, PIECES)),
            sem((count, PIECES)),
            sem((count, PIECES // GROUP)),
            sem((count, PIECES // GROUP)),
            sem((count, PIECES)),
        ],
        compiler_params=pltpu.CompilerParams(
            collective_id=0, has_side_effects=True, vmem_limit_bytes=62_200_000
        ),
        name="forward_substitution",
    )(rhs, jnp.swapaxes(panels_l, 1, 2), jnp.swapaxes(diag_inverse, 1, 2))


def solution(mesh):
    in_specs = (P("row", "col"), P(None, "row", "col"), P(None, None, "col"))
    out_specs = P("row", "col")
    return jax.shard_map(
        per_device, mesh=mesh, in_specs=in_specs, out_specs=out_specs, check_vma=False
    )
```

```python
import functools

import jax
import jax.numpy as jnp
from jax import lax
from jax.experimental import pallas as pl
from jax.experimental.pallas import tpu as pltpu
from jax.sharding import PartitionSpec as P

MESH = pl.DeviceIdType.MESH
F32, BF16 = jnp.float32, jnp.bfloat16

UNITS = 12
HEAD, EARLY = 3, 7
SLOTS = EARLY + 8
PIECES = 16
GROUP = 4
SPOTS = 8
S_FIRST, S_HOP, S_NUM, S_DEN = 32, 4, 5, 4
GO = 1
LAG = -(-(S_FIRST + 7 * S_HOP + 16) // 4)
SLACK = 11
TURNS = -(-max(UNITS + LAG, 2 * UNITS - 1 + SLACK) // 4)


def split(v):
    high = v.astype(BF16)
    return high, (v - high.astype(F32)).astype(BF16)


def kernel(
    rhs, pan, diag, out, share, solved, right3, left3,
    go_sem, io_sem, take_sem, l_recv, l_send, c_recv, c_send, b_recv, b_send, x_send, h_recv, h_send,
):
    row, col = lax.axis_index("row"), lax.axis_index("col")
    z, core = row // 2, row % 2
    y, x = col // 4, col % 4
    rows = out.shape[0]
    panel = solved.shape[1]
    slab = pan.shape[1]
    half_slab, half_panel = slab // 2, panel // 2
    piece = half_panel // PIECES
    sibling = row + 1 - 2 * core
    down = (row + 2 - 4 * core + 16) % 16
    up = (row - 2 + 4 * core + 16) % 16
    hops = jnp.where(core == 0, z, (8 - z) % 8)

    ys = [lax.rem(y + d, 4) for d in range(4)]
    xs = [lax.rem(x + d, 4) for d in range(4)]
    sources = [[4 * ys[ry] + xs[rx] for rx in range(4)] for ry in range(4)]
    starts = [[slab * v for v in line] for line in sources]

    def at_plane(dy, dx):
        return (row, sources[dy % 4][dx % 4])

    def relative(ry, rx):
        return (ry % 4) * 4 + rx % 4


    def tile_part(unit, part, ry, rx):
        start = starts[ry % 4][rx % 4] + (half_slab if part == 1 else 0)
        size = slab if part is None else half_slab
        return share.at[unit, pl.ds(pl.multiple_of(start, half_slab), size), :]

    def send(unit, part, src, to, slot):
        ref = tile_part(unit, part, *src)
        pltpu.make_async_remote_copy(
            src_ref=ref, dst_ref=ref,
            send_sem=l_send.at[unit, slot],
            recv_sem=l_recv.at[unit, part or 0, relative(src[0] - to[0], src[1] - to[1])],
            device_id=at_plane(*to), device_id_type=MESH,
        ).start()

    def arrive(unit, part, ry, rx):
        ref = tile_part(unit, part, ry, rx)
        pltpu.make_async_remote_copy(
            src_ref=ref, dst_ref=ref,
            send_sem=l_send.at[unit, 0],
            recv_sem=l_recv.at[unit, part or 0, relative(ry, rx)],
            device_id=at_plane(0, 1), device_id_type=MESH,
        ).wait_recv()

    def stage0(unit):
        for slot, to in enumerate(((0, 1), (0, -1), (1, 0), (-1, 0))):
            send(unit, None, (0, 0), to, slot)

    def stage1(unit, e, step):
        if step == 0:
            arrive(unit, None, 0, -e)
            send(unit, 0, (0, -e), (0, e), 4)
            send(unit, 0, (0, -e), (1, 0), 5)
            send(unit, 0, (0, -e), (-1, 0), 6)
        elif step == 1:
            arrive(unit, None, e, 0)
            send(unit, 1, (e, 0), (-e, 0), 7)
            send(unit, 1, (e, 0), (0, 1), 8)
            send(unit, 1, (e, 0), (0, -1), 9)
        elif step == 2:
            arrive(unit, None, 0, e)
            send(unit, 0, (0, e), (1, 0), 10)
            send(unit, 0, (0, e), (-1, 0), 11)
            send(unit, 1, (0, e), (0, -e), 12)
        else:
            arrive(unit, None, -e, 0)
            send(unit, 1, (-e, 0), (0, 1), 13)
            send(unit, 1, (-e, 0), (0, -1), 14)
            send(unit, 0, (-e, 0), (e, 0), 15)

    def stage2(unit, e, step):
        if step == 0:
            arrive(unit, 0, 0, 2)
            send(unit, 0, (0, 2), (1, 0), 16)
            send(unit, 0, (0, 2), (-1, 0), 17)
            arrive(unit, 1, 2, 0)
            send(unit, 1, (2, 0), (0, 1), 18)
            send(unit, 1, (2, 0), (0, -1), 19)
        elif step == 1:
            arrive(unit, 0, -e, 1)
            send(unit, 0, (-e, 1), (e, 0), 20)
            arrive(unit, 1, 1, e)
            send(unit, 1, (1, e), (0, -e), 21)
        else:
            arrive(unit, 0, -e, -1)
            send(unit, 0, (-e, -1), (e, 0), 22)
            arrive(unit, 1, -1, e)
            send(unit, 1, (-1, e), (0, -e), 23)

    def stage3(unit, e):
        arrive(unit, 0, -e, 2)
        send(unit, 0, (-e, 2), (e, 0), 24)
        arrive(unit, 1, 2, e)
        send(unit, 1, (2, e), (0, -e), 25)

    def final(unit):
        def rest(e):
            for ry, rx in ((e, 1), (e, -1), (2, 0), (e, 2), (2, 1), (2, -1), (2, 2)):
                arrive(unit, 0, ry, rx)
            for ry, rx in ((1, -e), (-1, -e), (0, 2), (2, -e), (1, 2), (-1, 2), (2, 2)):
                arrive(unit, 1, ry, rx)

        even = lax.rem(unit, 2) == 0
        pl.when(even)(lambda: rest(1))
        pl.when(jnp.logical_not(even))(lambda: rest(-1))

    def drain_shares(count):
        def body(unit, _):
            for slot in range(26):
                ref = tile_part(unit, None if slot < 4 else 0, 0, 0)
                pltpu.make_async_remote_copy(
                    src_ref=ref, dst_ref=ref,
                    send_sem=l_send.at[unit, slot], recv_sem=l_recv.at[unit, 0, 0],
                    device_id=at_plane(0, 1), device_id_type=MESH,
                ).wait_send()
            return 0

        lax.fori_loop(0, count, body, 0)


    def strip(k, which, p):
        start = pl.multiple_of(which * half_panel + p * piece, piece)
        return solved.at[k, pl.ds(start, piece), :]

    def hop(k, which, p, send_sem, recv_sem, to):
        ref = strip(k, which, p)
        return pltpu.make_async_remote_copy(
            src_ref=ref, dst_ref=ref, send_sem=send_sem.at[k, p], recv_sem=recv_sem.at[k, p],
            device_id=(to, col), device_id_type=MESH,
        )

    def relay(j, to_sibling):
        k, p = lax.div(j, PIECES), lax.rem(j, PIECES)
        hop(k, core, p, c_send, c_recv, up).wait_recv()

        @pl.when(hops < 7)
        def _():
            hop(k, core, p, c_send, c_recv, down).start()

        if to_sibling:

            @pl.when(lax.rem(p, GROUP) == GROUP - 1)
            def _():
                beside(k, core, lax.div(p, GROUP)).start()

    def beside(k, which, g):
        rows = GROUP * piece
        ref = solved.at[k, pl.ds(pl.multiple_of(which * half_panel + g * rows, rows), rows), :]
        return pltpu.make_async_remote_copy(
            src_ref=ref, dst_ref=ref, send_sem=b_send.at[k, g], recv_sem=b_recv.at[k, g],
            device_id=(sibling, col), device_id_type=MESH,
        )

    def from_sibling(k):
        for g in range(PIECES // GROUP):
            beside(k, 1 - core, g).wait_recv()


    def convert(src):
        def body(b, _):
            start = pl.multiple_of(b * 32, 32)
            high, low = split(src[pl.ds(start, 32), :])
            right3[pl.ds(start, 32), :] = high
            right3[pl.ds(pl.multiple_of(panel + start, 32), 32), :] = low
            right3[pl.ds(pl.multiple_of(2 * panel + start, 32), 32), :] = high
            return 0

        lax.fori_loop(0, panel // 32, body, 0)

    def unfold(unit):
        def body(b, _):
            start = pl.multiple_of(b * 128, 128)
            for g in range(panel // 128):
                tile = share[unit, pl.ds(start, 128), g * 128 : (g + 1) * 128].T
                high, low = split(tile)
                to = pl.ds(g * 128, 128)
                left3[to, pl.ds(start, 128)] = high
                left3[to, pl.ds(pl.multiple_of(panel + start, 128), 128)] = high
                left3[to, pl.ds(pl.multiple_of(2 * panel + start, 128), 128)] = low
            return 0

        lax.fori_loop(0, panel // 128, body, 0)

    def product(block, dest):
        cols = pl.ds(pl.multiple_of(block * 256, 256), 256)
        to = pl.ds(pl.multiple_of(dest * panel, panel), panel)
        acc = jnp.dot(left3[...], right3[:, cols], preferred_element_type=F32)
        return cols, to, acc

    def subtract(block, dest):
        cols, to, acc = product(block, dest)
        out[to, cols] = out[to, cols] - acc

    def assign(block, dest, k):
        cols, to, acc = product(block, dest)
        out[to, cols] = acc
        solved[k, :, cols] = acc

    def subtract_ahead(k):
        def body(block, _):
            cols, _, acc = product(block, 0)
            solved[k, :, cols] = solved[k, :, cols] - acc
            return 0

        lax.fori_loop(0, 3, body, 0)

    def assign_ahead(k):
        def body(block, _):
            cols, _, acc = product(block, 0)
            solved[k, :, cols] = acc
            return 0

        lax.fori_loop(0, 3, body, 0)

    def subtract_all(dest):
        def body(block, _):
            subtract(block, dest)
            return 0

        lax.fori_loop(0, 3, body, 0)

    def assign_all(dest, k):
        def body(block, _):
            assign(block, dest, k)
            return 0

        lax.fori_loop(0, 3, body, 0)

    def out_panel(u):
        return out.at[pl.ds(pl.multiple_of(u * panel, panel), panel), :]


    first, second = row == 0, row == 1

    def loop(first, last, body):
        def turn(i, _):
            body(i)
            return 0

        lax.fori_loop(first, last, turn, 0)

    fetch = pltpu.make_async_copy(rhs, out, io_sem.at[0])
    fetch.start()

    def mine(t):
        return share.at[t, pl.ds(pl.multiple_of(col * slab, slab), slab), :]

    def take_factor(t, k, u):
        columns = pl.ds(pl.multiple_of(u * panel, panel), panel)
        return pltpu.make_async_copy(pan.at[k, :, columns], mine(t), take_sem.at[t])

    def take_inverse(t, k):
        return pltpu.make_async_copy(diag.at[k], mine(t), take_sem.at[t])

    @pl.when(row > 1)
    def _():
        loop(0, UNITS, lambda t: take_factor(t, t // 3, t % 3).start())

    @pl.when(first)
    def _():
        take_inverse(0, 0).start()
        take_factor(1, 0, 1).start()
        take_inverse(2, 1).start()

    @pl.when(second)
    def _():
        take_factor(0, 0, 0).start()
        take_inverse(3, 2).start()
        take_factor(4, 1, 0).start()
        take_factor(5, 2, 0).start()
        take_inverse(6, 3).start()
        loop(0, 8, lambda j: take_factor(EARLY + j, lax.div(j, 2), 1 + lax.rem(j, 2)).start())

    def handed(i):
        columns = pl.ds(2 * panel, panel)
        src, dst = (
            (rhs.at[columns, :], solved.at[2]),
            (pan.at[0, :, columns], mine(1)),
            (pan.at[1, :, columns], mine(2)),
            (solved.at[2], solved.at[2]),
        )[i]
        return pltpu.make_async_remote_copy(
            src_ref=src, dst_ref=dst, send_sem=h_send.at[i], recv_sem=h_recv.at[i],
            device_id=(sibling, col), device_id_type=MESH,
        )

    barrier = pltpu.get_barrier_semaphore()
    for to in (at_plane(0, 1), at_plane(0, -1), at_plane(1, 0), at_plane(-1, 0), (sibling, col), (up, col), (down, col)):
        pl.semaphore_signal(barrier, inc=1, device_id=to, device_id_type=MESH)

    for pair in ((1, 2), (2, 1)):

        @pl.when(row == pair[0])
        def _():
            pl.semaphore_signal(barrier, inc=1, device_id=(pair[1], col), device_id_type=MESH)

    loop(0, jnp.where(first, HEAD, jnp.where(second, 1, UNITS)), lambda t: take_inverse(t, 0).wait())

    @pl.when(second)
    def _():
        loop(3, SLOTS, lambda t: take_inverse(t, 0).wait())

    pl.semaphore_wait(barrier, jnp.where((row == 1) | (row == 2), 8, 7))


    def plane_turn(m, first_unit, last_unit):
        @pl.when(m + 2 < last_unit)
        def _():
            stage0(m + 2)

        def relays(e):
            @pl.when(m < last_unit)
            def _():
                for i in range(4):
                    stage1(m, e, i)

            @pl.when((m >= first_unit + 1) & (m < last_unit + 1))
            def _():
                for i in range(3):
                    stage2(m - 1, -e, i)

            @pl.when((m >= first_unit + 2) & (m < last_unit + 2))
            def _():
                stage3(m - 2, e)

        even = lax.rem(m, 2) == 0
        pl.when(even)(lambda: relays(1))
        pl.when(jnp.logical_not(even))(lambda: relays(-1))

    @pl.when(first)
    def _():
        for i in (1, 2):
            handed(i).start()
        stage0(0)
        stage0(1)
        handed(0).start()

        def turn(m):
            @pl.when(m == GO)
            def _():
                pl.semaphore_signal(go_sem, inc=1, device_id=(sibling, col), device_id_type=MESH)

            plane_turn(m, 0, HEAD)

            @pl.when(m == 3)
            def _():
                fetch.wait()

            @pl.when(m >= 3)
            def _():
                q = m - 3
                final(q)
                k = jnp.where(q < 2, 0, 1)
                convert(out_panel(k))
                unfold(q)

                @pl.when(q != 1)
                def _():
                    assign_all(k, k)
                    for p in range(PIECES):
                        hop(k, 0, p, c_send, c_recv, down).start()
                        hop(k, 1, p, x_send, c_recv, sibling).start()
                    for g in range(PIECES // GROUP):
                        beside(k, 0, g).start()

                @pl.when(q == 1)
                def _():
                    subtract_all(1)

        loop(0, HEAD + 3, turn)
        handed(3).wait_recv()
        back = pltpu.make_async_copy(solved.at[2], out.at[pl.ds(2 * panel, panel), :], io_sem.at[0])
        back.start()
        drain_shares(HEAD)

        def drain(j):
            k, p = lax.div(j, PIECES), lax.rem(j, PIECES)
            hop(k, 0, p, c_send, c_recv, down).wait_send()
            hop(k, 1, p, x_send, c_recv, sibling).wait_send()

            @pl.when(lax.rem(p, GROUP) == 0)
            def _():
                beside(k, 0, lax.div(p, GROUP)).wait_send()

        loop(0, 2 * PIECES, drain)
        for i in range(3):
            handed(i).wait_send()
        back.wait()

    @pl.when(second)
    def _():
        pl.semaphore_wait(go_sem, 1)
        stage0(0)
        for i in (1, 2):
            handed(i).wait_recv()
        stage0(1)

        def pass_on(k):
            for p in range(PIECES):
                hop(k, 1, p, c_send, c_recv, down).start()
                hop(k, 0, p, x_send, c_recv, 2).start()

        def early_turn(m):
            plane_turn(m, 0, SLOTS)

            @pl.when(m >= 3)
            def _():
                q = m - 3
                final(q)

                @pl.when((q == 0) | (q == 2))
                def _():
                    k = lax.div(q, 2)
                    loop(k * PIECES, (k + 1) * PIECES, lambda j: relay(j, False))
                    from_sibling(k)

                @pl.when(q == 0)
                def _():
                    fetch.wait()

                @pl.when(q == 1)
                def _():
                    handed(0).wait_recv()

                @pl.when(q == 6)
                def _():
                    convert(out_panel(0))

                @pl.when((q != 1) & (q != 6))
                def _():
                    convert(solved.at[jnp.where(q == 0, 0, jnp.where((q == 2) | (q == 4), 1, 2))])

                unfold(q)

                @pl.when((q == 0) | (q == 4) | (q == 5))
                def _():
                    subtract_all(0)

                @pl.when((q == 1) | (q == 2))
                def _():
                    subtract_ahead(2)

                @pl.when(q == 3)
                def _():
                    assign_ahead(2)
                    pass_on(2)
                    handed(3).start()

                @pl.when(q == 6)
                def _():
                    assign_all(0, 3)
                    pass_on(3)

        loop(0, EARLY + 3, early_turn)
        def turn(m):
            plane_turn(m, 0, SLOTS)

            @pl.when(m >= EARLY + 3)
            def _():
                q = m - 3
                j = q - EARLY
                final(q)

                @pl.when(lax.rem(j, 2) == 0)
                def _():
                    convert(solved.at[lax.div(j, 2)])

                unfold(q)
                subtract_all(1 + lax.rem(j, 2))

        loop(EARLY + 3, SLOTS + 3, turn)
        drain_shares(SLOTS)
        loop(0, 4 * PIECES, lambda j: hop(lax.div(j, PIECES), 1, lax.rem(j, PIECES), c_send, c_recv, down).wait_send())
        loop(2 * PIECES, 4 * PIECES, lambda j: hop(lax.div(j, PIECES), 0, lax.rem(j, PIECES), x_send, c_recv, 2).wait_send())
        handed(3).wait_send()


    @pl.when(row > 1)
    def _():
        farthest = jnp.maximum(hops, 8 - hops)
        lag = lax.div(S_FIRST + S_HOP * farthest + 16 + 3, 4)
        due = S_FIRST + S_HOP * hops

        def relayed(spot):
            ahead = jnp.maximum(spot - due, 0)
            return jnp.minimum(lax.div(ahead * S_NUM, S_DEN), 4 * PIECES)

        def taken(slot):
            ready = jnp.minimum(slot - lag + 1, lax.div(jnp.maximum(slot - SLACK + 2, 0), 2))
            return jnp.clip(ready, 0, UNITS)

        stage0(0)
        stage0(1)

        def tile_turn(m, e, carry):
            before, done = carry
            for i in range(SPOTS):
                if i == 0:

                    @pl.when(m + 2 < UNITS)
                    def _():
                        stage0(m + 2)

                if i % 2 == 0:

                    @pl.when(m < UNITS)
                    def _():
                        stage1(m, e, i // 2)
                elif i < 7:

                    @pl.when((m >= 2) & (m < UNITS + 2))
                    def _():
                        stage2(m - 2, e, i // 2)
                else:

                    @pl.when((m >= 3) & (m < UNITS + 3))
                    def _():
                        stage3(m - 3, -e)

                now = relayed(m * SPOTS + i)
                loop(done, now, lambda j: relay(j, True))
                done = now

                part = i % 4
                if part == 0:
                    after = taken(2 * m + i // 4)
                    q = after - 1
                    k, u = lax.div(jnp.maximum(q, 0), 3), lax.rem(jnp.maximum(q, 0), 3)
                    fresh = after > before
                    before = after

                    @pl.when(fresh)
                    def _():
                        final(q)

                        @pl.when(q == 0)
                        def _():
                            fetch.wait()

                        @pl.when(u == 0)
                        def _():
                            from_sibling(k)
                            convert(solved.at[k])

                        unfold(q)
                else:

                    @pl.when(fresh)
                    def _():
                        subtract(part - 1, u)

            return before, done

        def turn(t, carry):
            carry = tile_turn(2 * t, 1, carry)
            return tile_turn(2 * t + 1, -1, carry)

        lax.fori_loop(0, TURNS, turn, (jnp.int32(0), jnp.int32(0)))
        drain_shares(UNITS)

        def drain(j):
            k, p = j // PIECES, j % PIECES

            @pl.when(hops < 7)
            def _():
                hop(k, core, p, c_send, c_recv, down).wait_send()

            @pl.when(lax.rem(p, GROUP) == 0)
            def _():
                beside(k, core, lax.div(p, GROUP)).wait_send()

        loop(0, 4 * PIECES, drain)


def per_device(rhs, panels_l, diag_inverse):
    rows, width = rhs.shape
    count, panel, _ = diag_inverse.shape
    sem = pltpu.SemaphoreType.DMA
    return pl.pallas_call(
        kernel,
        out_shape=pltpu.VMEM((rows, width), F32),
        in_specs=[pl.BlockSpec(memory_space=pl.ANY)] * 3,
        out_specs=pl.BlockSpec(memory_space=pltpu.VMEM),
        scratch_shapes=[
            pltpu.VMEM((SLOTS, panel, panel), F32),
            pltpu.VMEM((count, panel, width), F32),
            pltpu.VMEM((3 * panel, width), BF16),
            pltpu.VMEM((panel, 3 * panel), BF16),
            pltpu.SemaphoreType.REGULAR,
            sem((1,)),
            sem((SLOTS,)),
            sem((SLOTS, 2, 16)),
            sem((SLOTS, 26)),
            sem((count, PIECES)),
            sem((count, PIECES)),
            sem((count, PIECES // GROUP)),
            sem((count, PIECES // GROUP)),
            sem((count, PIECES)),
            sem((4,)),
            sem((4,)),
        ],
        compiler_params=pltpu.CompilerParams(
            collective_id=0, has_side_effects=True, vmem_limit_bytes=62_200_000
        ),
        name="forward_substitution",
    )(rhs, jnp.swapaxes(panels_l, 1, 2), jnp.swapaxes(diag_inverse, 1, 2))


def solution(mesh):
    in_specs = (P("row", "col"), P(None, "row", "col"), P(None, None, "col"))
    out_specs = P("row", "col")
    return jax.shard_map(
        per_device, mesh=mesh, in_specs=in_specs, out_specs=out_specs, check_vma=False
    )
```

```python
import functools

import jax
import jax.numpy as jnp
from jax import lax
from jax.experimental import pallas as pl
from jax.experimental.pallas import tpu as pltpu
from jax.sharding import PartitionSpec as P

MESH = pl.DeviceIdType.MESH
F32, BF16 = jnp.float32, jnp.bfloat16

UNITS = 12
HEAD, EARLY = 3, 7
SLOTS = EARLY + 8
PIECES = 16
GROUP = 4
SPOTS = 8
S_FIRST, S_HOP, S_NUM, S_DEN = 32, 5, 5, 4
GO = 1
LAG = -(-(S_FIRST + 7 * S_HOP + 16) // 4)
SLACK = 11
TURNS = -(-max(UNITS + LAG, 2 * UNITS - 1 + SLACK) // 4)


def split(v):
    high = v.astype(BF16)
    return high, (v - high.astype(F32)).astype(BF16)


def kernel(
    rhs, pan, diag, out, share, solved, right3, left3,
    go_sem, io_sem, take_sem, l_recv, l_send, c_recv, c_send, b_recv, b_send, x_send, h_recv, h_send,
):
    row, col = lax.axis_index("row"), lax.axis_index("col")
    z, core = row // 2, row % 2
    y, x = col // 4, col % 4
    rows = out.shape[0]
    panel = solved.shape[1]
    slab = pan.shape[1]
    half_slab, half_panel = slab // 2, panel // 2
    piece = half_panel // PIECES
    sibling = row + 1 - 2 * core
    down = (row + 2 - 4 * core + 16) % 16
    up = (row - 2 + 4 * core + 16) % 16
    hops = jnp.where(core == 0, z, (8 - z) % 8)

    ys = [lax.rem(y + d, 4) for d in range(4)]
    xs = [lax.rem(x + d, 4) for d in range(4)]
    sources = [[4 * ys[ry] + xs[rx] for rx in range(4)] for ry in range(4)]
    starts = [[slab * v for v in line] for line in sources]

    def at_plane(dy, dx):
        return (row, sources[dy % 4][dx % 4])

    def relative(ry, rx):
        return (ry % 4) * 4 + rx % 4


    def tile_part(unit, part, ry, rx):
        start = starts[ry % 4][rx % 4] + (half_slab if part == 1 else 0)
        size = slab if part is None else half_slab
        return share.at[unit, pl.ds(pl.multiple_of(start, half_slab), size), :]

    def send(unit, part, src, to, slot):
        ref = tile_part(unit, part, *src)
        pltpu.make_async_remote_copy(
            src_ref=ref, dst_ref=ref,
            send_sem=l_send.at[unit, slot],
            recv_sem=l_recv.at[unit, part or 0, relative(src[0] - to[0], src[1] - to[1])],
            device_id=at_plane(*to), device_id_type=MESH,
        ).start()

    def arrive(unit, part, ry, rx):
        ref = tile_part(unit, part, ry, rx)
        pltpu.make_async_remote_copy(
            src_ref=ref, dst_ref=ref,
            send_sem=l_send.at[unit, 0],
            recv_sem=l_recv.at[unit, part or 0, relative(ry, rx)],
            device_id=at_plane(0, 1), device_id_type=MESH,
        ).wait_recv()

    def stage0(unit):
        for slot, to in enumerate(((0, 1), (0, -1), (1, 0), (-1, 0))):
            send(unit, None, (0, 0), to, slot)

    def stage1(unit, e, step):
        if step == 0:
            arrive(unit, None, 0, -e)
            send(unit, 0, (0, -e), (0, e), 4)
            send(unit, 0, (0, -e), (1, 0), 5)
            send(unit, 0, (0, -e), (-1, 0), 6)
        elif step == 1:
            arrive(unit, None, e, 0)
            send(unit, 1, (e, 0), (-e, 0), 7)
            send(unit, 1, (e, 0), (0, 1), 8)
            send(unit, 1, (e, 0), (0, -1), 9)
        elif step == 2:
            arrive(unit, None, 0, e)
            send(unit, 0, (0, e), (1, 0), 10)
            send(unit, 0, (0, e), (-1, 0), 11)
            send(unit, 1, (0, e), (0, -e), 12)
        else:
            arrive(unit, None, -e, 0)
            send(unit, 1, (-e, 0), (0, 1), 13)
            send(unit, 1, (-e, 0), (0, -1), 14)
            send(unit, 0, (-e, 0), (e, 0), 15)

    def stage2(unit, e, step):
        if step == 0:
            arrive(unit, 0, 0, 2)
            send(unit, 0, (0, 2), (1, 0), 16)
            send(unit, 0, (0, 2), (-1, 0), 17)
            arrive(unit, 1, 2, 0)
            send(unit, 1, (2, 0), (0, 1), 18)
            send(unit, 1, (2, 0), (0, -1), 19)
        elif step == 1:
            arrive(unit, 0, -e, 1)
            send(unit, 0, (-e, 1), (e, 0), 20)
            arrive(unit, 1, 1, e)
            send(unit, 1, (1, e), (0, -e), 21)
        else:
            arrive(unit, 0, -e, -1)
            send(unit, 0, (-e, -1), (e, 0), 22)
            arrive(unit, 1, -1, e)
            send(unit, 1, (-1, e), (0, -e), 23)

    def stage3(unit, e):
        arrive(unit, 0, -e, 2)
        send(unit, 0, (-e, 2), (e, 0), 24)
        arrive(unit, 1, 2, e)
        send(unit, 1, (2, e), (0, -e), 25)

    def final(unit):
        def rest(e):
            for ry, rx in ((e, 1), (e, -1), (2, 0), (e, 2), (2, 1), (2, -1), (2, 2)):
                arrive(unit, 0, ry, rx)
            for ry, rx in ((1, -e), (-1, -e), (0, 2), (2, -e), (1, 2), (-1, 2), (2, 2)):
                arrive(unit, 1, ry, rx)

        even = lax.rem(unit, 2) == 0
        pl.when(even)(lambda: rest(1))
        pl.when(jnp.logical_not(even))(lambda: rest(-1))

    def drain_shares(count):
        def body(unit, _):
            for slot in range(26):
                ref = tile_part(unit, None if slot < 4 else 0, 0, 0)
                pltpu.make_async_remote_copy(
                    src_ref=ref, dst_ref=ref,
                    send_sem=l_send.at[unit, slot], recv_sem=l_recv.at[unit, 0, 0],
                    device_id=at_plane(0, 1), device_id_type=MESH,
                ).wait_send()
            return 0

        lax.fori_loop(0, count, body, 0)


    def strip(k, which, p):
        start = pl.multiple_of(which * half_panel + p * piece, piece)
        return solved.at[k, pl.ds(start, piece), :]

    def hop(k, which, p, send_sem, recv_sem, to):
        ref = strip(k, which, p)
        return pltpu.make_async_remote_copy(
            src_ref=ref, dst_ref=ref, send_sem=send_sem.at[k, p], recv_sem=recv_sem.at[k, p],
            device_id=(to, col), device_id_type=MESH,
        )

    def relay(j, to_sibling):
        k, p = lax.div(j, PIECES), lax.rem(j, PIECES)
        hop(k, core, p, c_send, c_recv, up).wait_recv()

        @pl.when(hops < 7)
        def _():
            hop(k, core, p, c_send, c_recv, down).start()

        if to_sibling:

            @pl.when(lax.rem(p, GROUP) == GROUP - 1)
            def _():
                beside(k, core, lax.div(p, GROUP)).start()

    def beside(k, which, g):
        rows = GROUP * piece
        ref = solved.at[k, pl.ds(pl.multiple_of(which * half_panel + g * rows, rows), rows), :]
        return pltpu.make_async_remote_copy(
            src_ref=ref, dst_ref=ref, send_sem=b_send.at[k, g], recv_sem=b_recv.at[k, g],
            device_id=(sibling, col), device_id_type=MESH,
        )

    def from_sibling(k):
        for g in range(PIECES // GROUP):
            beside(k, 1 - core, g).wait_recv()


    def convert(src):
        def body(b, _):
            start = pl.multiple_of(b * 32, 32)
            high, low = split(src[pl.ds(start, 32), :])
            right3[pl.ds(start, 32), :] = high
            right3[pl.ds(pl.multiple_of(panel + start, 32), 32), :] = low
            right3[pl.ds(pl.multiple_of(2 * panel + start, 32), 32), :] = high
            return 0

        lax.fori_loop(0, panel // 32, body, 0)

    def unfold(unit):
        def body(b, _):
            start = pl.multiple_of(b * 128, 128)
            for g in range(panel // 128):
                tile = share[unit, pl.ds(start, 128), g * 128 : (g + 1) * 128].T
                high, low = split(tile)
                to = pl.ds(g * 128, 128)
                left3[to, pl.ds(start, 128)] = high
                left3[to, pl.ds(pl.multiple_of(panel + start, 128), 128)] = high
                left3[to, pl.ds(pl.multiple_of(2 * panel + start, 128), 128)] = low
            return 0

        lax.fori_loop(0, panel // 128, body, 0)

    def product(block, dest):
        cols = pl.ds(pl.multiple_of(block * 256, 256), 256)
        to = pl.ds(pl.multiple_of(dest * panel, panel), panel)
        acc = jnp.dot(left3[...], right3[:, cols], preferred_element_type=F32)
        return cols, to, acc

    def subtract(block, dest):
        cols, to, acc = product(block, dest)
        out[to, cols] = out[to, cols] - acc

    def assign(block, dest, k):
        cols, to, acc = product(block, dest)
        out[to, cols] = acc
        solved[k, :, cols] = acc


    half3 = 3 * half_panel

    def convert_half(k, which, turn):
        def body(b, _):
            start = pl.multiple_of(b * 32, 32)
            high, low = split(solved[k, pl.ds(pl.multiple_of(which * half_panel + start, 32), 32), :])
            for i, v in enumerate((high, low, high)):
                right3[pl.ds(pl.multiple_of(turn * half3 + i * half_panel + start, 32), 32), :] = v
            return 0

        lax.fori_loop(0, half_panel // 32, body, 0)

    def unfold_half(unit, which):
        for b in range(half_panel // 128):
            start = pl.multiple_of(which * half_panel + b * 128, 128)
            for g in range(panel // 128):
                high, low = split(share[unit, pl.ds(start, 128), g * 128 : (g + 1) * 128].T)
                for i, v in enumerate((high, high, low)):
                    left3[g * 128 : (g + 1) * 128, i * half_panel + b * 128 : i * half_panel + (b + 1) * 128] = v

    def subtract_half(block, dest, turn):
        cols = pl.ds(block * 256, 256)
        to = pl.ds(pl.multiple_of(dest * panel, panel), panel)
        acc = jnp.dot(left3[:, :half3], right3[turn * half3 : (turn + 1) * half3, cols], preferred_element_type=F32)
        out[to, cols] = out[to, cols] - acc

    def subtract_ahead(k):
        def body(block, _):
            cols, _, acc = product(block, 0)
            solved[k, :, cols] = solved[k, :, cols] - acc
            return 0

        lax.fori_loop(0, 3, body, 0)

    def assign_ahead(k):
        def body(block, _):
            cols, _, acc = product(block, 0)
            solved[k, :, cols] = acc
            return 0

        lax.fori_loop(0, 3, body, 0)

    def subtract_all(dest):
        def body(block, _):
            subtract(block, dest)
            return 0

        lax.fori_loop(0, 3, body, 0)

    def assign_all(dest, k):
        def body(block, _):
            assign(block, dest, k)
            return 0

        lax.fori_loop(0, 3, body, 0)

    def out_panel(u):
        return out.at[pl.ds(pl.multiple_of(u * panel, panel), panel), :]


    first, second = row == 0, row == 1

    def loop(first, last, body):
        def turn(i, _):
            body(i)
            return 0

        lax.fori_loop(first, last, turn, 0)

    fetch = pltpu.make_async_copy(rhs, out, io_sem.at[0])

    def mine(t):
        return share.at[t, pl.ds(pl.multiple_of(col * slab, slab), slab), :]

    def take_factor(t, k, u):
        columns = pl.ds(pl.multiple_of(u * panel, panel), panel)
        return pltpu.make_async_copy(pan.at[k, :, columns], mine(t), take_sem.at[t])

    def take_inverse(t, k):
        return pltpu.make_async_copy(diag.at[k], mine(t), take_sem.at[t])

    @pl.when(row > 1)
    def _():
        loop(0, UNITS, lambda t: take_factor(t, t // 3, t % 3).start())

    @pl.when(first)
    def _():
        take_inverse(0, 0).start()
        take_factor(1, 0, 1).start()
        take_inverse(2, 1).start()

    @pl.when(second)
    def _():
        take_factor(0, 0, 0).start()
        take_inverse(3, 2).start()
        take_factor(4, 1, 0).start()
        take_factor(5, 2, 0).start()
        take_inverse(6, 3).start()
        loop(0, 8, lambda j: take_factor(EARLY + j, lax.div(j, 2), 1 + lax.rem(j, 2)).start())

    def handed(i):
        columns = pl.ds(2 * panel, panel)
        src, dst = (
            (rhs.at[columns, :], solved.at[2]),
            (pan.at[0, :, columns], mine(1)),
            (pan.at[1, :, columns], mine(2)),
            (solved.at[2], solved.at[2]),
        )[i]
        return pltpu.make_async_remote_copy(
            src_ref=src, dst_ref=dst, send_sem=h_send.at[i], recv_sem=h_recv.at[i],
            device_id=(sibling, col), device_id_type=MESH,
        )

    barrier = pltpu.get_barrier_semaphore()
    for to in (at_plane(0, 1), at_plane(0, -1), at_plane(1, 0), at_plane(-1, 0), (sibling, col), (up, col), (down, col)):
        pl.semaphore_signal(barrier, inc=1, device_id=to, device_id_type=MESH)

    for pair in ((1, 2), (2, 1)):

        @pl.when(row == pair[0])
        def _():
            pl.semaphore_signal(barrier, inc=1, device_id=(pair[1], col), device_id_type=MESH)

    loop(0, jnp.where(first, HEAD, jnp.where(second, 1, UNITS)), lambda t: take_inverse(t, 0).wait())

    @pl.when(second)
    def _():
        loop(3, SLOTS, lambda t: take_inverse(t, 0).wait())

    fetch.start()
    pl.semaphore_wait(barrier, jnp.where((row == 1) | (row == 2), 8, 7))


    def plane_turn(m, first_unit, last_unit):
        @pl.when(m + 2 < last_unit)
        def _():
            stage0(m + 2)

        def relays(e):
            @pl.when(m < last_unit)
            def _():
                for i in range(4):
                    stage1(m, e, i)

            @pl.when((m >= first_unit + 1) & (m < last_unit + 1))
            def _():
                for i in range(3):
                    stage2(m - 1, -e, i)

            @pl.when((m >= first_unit + 2) & (m < last_unit + 2))
            def _():
                stage3(m - 2, e)

        even = lax.rem(m, 2) == 0
        pl.when(even)(lambda: relays(1))
        pl.when(jnp.logical_not(even))(lambda: relays(-1))

    @pl.when(first)
    def _():
        for i in (1, 2):
            handed(i).start()
        stage0(0)
        stage0(1)
        handed(0).start()

        def turn(m):
            @pl.when(m == GO)
            def _():
                pl.semaphore_signal(go_sem, inc=1, device_id=(sibling, col), device_id_type=MESH)

            plane_turn(m, 0, HEAD)

            @pl.when(m == 3)
            def _():
                fetch.wait()

            @pl.when(m >= 3)
            def _():
                q = m - 3
                final(q)
                k = jnp.where(q < 2, 0, 1)
                convert(out_panel(k))
                unfold(q)

                @pl.when(q != 1)
                def _():
                    assign_all(k, k)
                    for p in range(PIECES):
                        hop(k, 0, p, c_send, c_recv, down).start()
                        hop(k, 1, p, x_send, c_recv, sibling).start()
                    for g in range(PIECES // GROUP):
                        beside(k, 0, g).start()

                @pl.when(q == 1)
                def _():
                    subtract_all(1)

        loop(0, HEAD + 3, turn)
        handed(3).wait_recv()
        back = pltpu.make_async_copy(solved.at[2], out.at[pl.ds(2 * panel, panel), :], io_sem.at[0])
        back.start()
        drain_shares(HEAD)

        def drain(j):
            k, p = lax.div(j, PIECES), lax.rem(j, PIECES)
            hop(k, 0, p, c_send, c_recv, down).wait_send()
            hop(k, 1, p, x_send, c_recv, sibling).wait_send()

            @pl.when(lax.rem(p, GROUP) == 0)
            def _():
                beside(k, 0, lax.div(p, GROUP)).wait_send()

        loop(0, 2 * PIECES, drain)
        for i in range(3):
            handed(i).wait_send()
        back.wait()

    @pl.when(second)
    def _():
        pl.semaphore_wait(go_sem, 1)
        stage0(0)
        for i in (1, 2):
            handed(i).wait_recv()
        stage0(1)

        def pass_on(k):
            for p in range(PIECES):
                hop(k, 1, p, c_send, c_recv, down).start()
                hop(k, 0, p, x_send, c_recv, 2).start()

        def early_turn(m):
            plane_turn(m, 0, SLOTS)

            @pl.when(m >= 3)
            def _():
                q = m - 3
                final(q)
                unfold(q)

                @pl.when((q == 0) | (q == 2))
                def _():
                    k = lax.div(q, 2)
                    loop(k * PIECES, (k + 1) * PIECES, lambda j: relay(j, False))
                    from_sibling(k)

                @pl.when(q == 0)
                def _():
                    fetch.wait()

                @pl.when(q == 1)
                def _():
                    handed(0).wait_recv()

                @pl.when(q == 6)
                def _():
                    convert(out_panel(0))

                @pl.when((q != 1) & (q != 6))
                def _():
                    convert(solved.at[jnp.where(q == 0, 0, jnp.where((q == 2) | (q == 4), 1, 2))])

                @pl.when((q == 0) | (q == 4) | (q == 5))
                def _():
                    subtract_all(0)

                @pl.when((q == 1) | (q == 2))
                def _():
                    subtract_ahead(2)

                @pl.when(q == 3)
                def _():
                    assign_ahead(2)
                    pass_on(2)
                    handed(3).start()

                @pl.when(q == 6)
                def _():
                    assign_all(0, 3)
                    pass_on(3)

        loop(0, EARLY + 3, early_turn)
        def turn(m):
            plane_turn(m, 0, SLOTS)

            @pl.when(m >= EARLY + 3)
            def _():
                q = m - 3
                j = q - EARLY
                final(q)

                @pl.when(lax.rem(j, 2) == 0)
                def _():
                    convert(solved.at[lax.div(j, 2)])

                unfold(q)
                subtract_all(1 + lax.rem(j, 2))

        loop(EARLY + 3, SLOTS + 3, turn)
        drain_shares(SLOTS)
        loop(0, 4 * PIECES, lambda j: hop(lax.div(j, PIECES), 1, lax.rem(j, PIECES), c_send, c_recv, down).wait_send())
        loop(2 * PIECES, 4 * PIECES, lambda j: hop(lax.div(j, PIECES), 0, lax.rem(j, PIECES), x_send, c_recv, 2).wait_send())
        handed(3).wait_send()


    @pl.when(row > 1)
    def _():
        near = hops <= 4
        halves = (jnp.where(near, core, 1 - core), jnp.where(near, 1 - core, core))
        lags = [
            lax.div(S_FIRST + S_HOP * h + 16 + 3, 4)
            for h in (jnp.minimum(hops, 8 - hops), jnp.maximum(hops, 8 - hops))
        ]
        due = S_FIRST + S_HOP * hops

        def relayed(spot):
            ahead = jnp.maximum(spot - due, 0)
            return jnp.minimum(lax.div(ahead * S_NUM, S_DEN), 4 * PIECES)

        def taken(slot, lag):
            ready = jnp.minimum(slot - lag + 1, lax.div(jnp.maximum(slot - SLACK + 2, 0), 2))
            return jnp.clip(ready, 0, UNITS)

        stage0(0)
        stage0(1)

        def tile_turn(m, e, carry):
            before, done = list(carry[:2]), carry[2]
            for i in range(SPOTS):
                if i == 0:

                    @pl.when(m + 2 < UNITS)
                    def _():
                        stage0(m + 2)

                if i % 2 == 0:

                    @pl.when(m < UNITS)
                    def _():
                        stage1(m, e, i // 2)
                elif i < 7:

                    @pl.when((m >= 2) & (m < UNITS + 2))
                    def _():
                        stage2(m - 2, e, i // 2)
                else:

                    @pl.when((m >= 3) & (m < UNITS + 3))
                    def _():
                        stage3(m - 3, -e)

                now = relayed(m * SPOTS + i)
                loop(done, now, lambda j: relay(j, True))
                done = now

                turn = (i % 4) // 2
                if i % 2 == 0:
                    after = taken(2 * m + i // 4, lags[turn])
                    q = after - 1
                    k, u = lax.div(jnp.maximum(q, 0), 3), lax.rem(jnp.maximum(q, 0), 3)
                    fresh = after > before[turn]
                    before[turn] = after

                    @pl.when(fresh)
                    def _():
                        if turn == 0:
                            final(q)

                            @pl.when(q == 0)
                            def _():
                                fetch.wait()

                        @pl.when(u == 0)
                        def _():
                            pl.when(near if turn == 1 else jnp.logical_not(near))(lambda: from_sibling(k))
                            convert_half(k, halves[turn], turn)

                        unfold_half(q, halves[turn])
                        subtract_half(0, u, turn)
                else:

                    @pl.when(fresh)
                    def _():
                        subtract_half(1, u, turn)
                        subtract_half(2, u, turn)

            return before[0], before[1], done

        def turn(t, carry):
            carry = tile_turn(2 * t, 1, carry)
            return tile_turn(2 * t + 1, -1, carry)

        lax.fori_loop(0, TURNS, turn, (jnp.int32(0),) * 3)
        drain_shares(UNITS)

        def drain(j):
            k, p = j // PIECES, j % PIECES

            @pl.when(hops < 7)
            def _():
                hop(k, core, p, c_send, c_recv, down).wait_send()

            @pl.when(lax.rem(p, GROUP) == 0)
            def _():
                beside(k, core, lax.div(p, GROUP)).wait_send()

        loop(0, 4 * PIECES, drain)


def per_device(rhs, panels_l, diag_inverse):
    rows, width = rhs.shape
    count, panel, _ = diag_inverse.shape
    sem = pltpu.SemaphoreType.DMA
    return pl.pallas_call(
        kernel,
        out_shape=pltpu.VMEM((rows, width), F32),
        in_specs=[pl.BlockSpec(memory_space=pl.ANY)] * 3,
        out_specs=pl.BlockSpec(memory_space=pltpu.VMEM),
        scratch_shapes=[
            pltpu.VMEM((SLOTS, panel, panel), F32),
            pltpu.VMEM((count, panel, width), F32),
            pltpu.VMEM((3 * panel, width), BF16),
            pltpu.VMEM((panel, 3 * panel), BF16),
            pltpu.SemaphoreType.REGULAR,
            sem((1,)),
            sem((SLOTS,)),
            sem((SLOTS, 2, 16)),
            sem((SLOTS, 26)),
            sem((count, PIECES)),
            sem((count, PIECES)),
            sem((count, PIECES // GROUP)),
            sem((count, PIECES // GROUP)),
            sem((count, PIECES)),
            sem((4,)),
            sem((4,)),
        ],
        compiler_params=pltpu.CompilerParams(
            collective_id=0, has_side_effects=True, vmem_limit_bytes=62_200_000
        ),
        name="forward_substitution",
    )(rhs, jnp.swapaxes(panels_l, 1, 2), jnp.swapaxes(diag_inverse, 1, 2))


def solution(mesh):
    in_specs = (P("row", "col"), P(None, "row", "col"), P(None, None, "col"))
    out_specs = P("row", "col")
    return jax.shard_map(
        per_device, mesh=mesh, in_specs=in_specs, out_specs=out_specs, check_vma=False
    )
```

```python
import functools

import jax
import jax.numpy as jnp
from jax import lax
from jax.experimental import pallas as pl
from jax.experimental.pallas import tpu as pltpu
from jax.sharding import PartitionSpec as P

MESH = pl.DeviceIdType.MESH
F32, BF16 = jnp.float32, jnp.bfloat16

UNITS = 12
HEAD, EARLY = 3, 7
SLOTS = EARLY + 8
PIECES = 16
GROUP = 4
SPOTS = 8
S_FIRST, S_HOP, S_NUM, S_DEN = 32, 5, 5, 4
GO = 1
LAG = -(-(S_FIRST + 7 * S_HOP + 16) // 4)
SLACK = 11
TURNS = -(-max(UNITS + LAG, 2 * UNITS - 1 + SLACK) // 4)


def split(v):
    high = v.astype(BF16)
    return high, (v - high.astype(F32)).astype(BF16)


def kernel(
    rhs, pan, diag, out, share, solved, right3, left3,
    go_sem, io_sem, take_sem, l_recv, l_send, c_recv, c_send, b_recv, b_send, x_send, h_recv, h_send,
):
    row, col = lax.axis_index("row"), lax.axis_index("col")
    z, core = row // 2, row % 2
    y, x = col // 4, col % 4
    rows = out.shape[0]
    panel = solved.shape[1]
    slab = pan.shape[1]
    half_slab, half_panel = slab // 2, panel // 2
    piece = half_panel // PIECES
    sibling = row + 1 - 2 * core
    down = (row + 2 - 4 * core + 16) % 16
    up = (row - 2 + 4 * core + 16) % 16
    hops = jnp.where(core == 0, z, (8 - z) % 8)

    ys = [lax.rem(y + d, 4) for d in range(4)]
    xs = [lax.rem(x + d, 4) for d in range(4)]
    sources = [[4 * ys[ry] + xs[rx] for rx in range(4)] for ry in range(4)]
    starts = [[slab * v for v in line] for line in sources]

    def at_plane(dy, dx):
        return (row, sources[dy % 4][dx % 4])

    def relative(ry, rx):
        return (ry % 4) * 4 + rx % 4


    def tile_part(unit, part, ry, rx):
        start = starts[ry % 4][rx % 4] + (half_slab if part == 1 else 0)
        size = slab if part is None else half_slab
        return share.at[unit, pl.ds(pl.multiple_of(start, half_slab), size), :]

    def send(unit, part, src, to, slot):
        ref = tile_part(unit, part, *src)
        pltpu.make_async_remote_copy(
            src_ref=ref, dst_ref=ref,
            send_sem=l_send.at[unit, slot],
            recv_sem=l_recv.at[unit, part or 0, relative(src[0] - to[0], src[1] - to[1])],
            device_id=at_plane(*to), device_id_type=MESH,
        ).start()

    def arrive(unit, part, ry, rx):
        ref = tile_part(unit, part, ry, rx)
        pltpu.make_async_remote_copy(
            src_ref=ref, dst_ref=ref,
            send_sem=l_send.at[unit, 0],
            recv_sem=l_recv.at[unit, part or 0, relative(ry, rx)],
            device_id=at_plane(0, 1), device_id_type=MESH,
        ).wait_recv()

    def stage0(unit):
        for slot, to in enumerate(((0, 1), (0, -1), (1, 0), (-1, 0))):
            send(unit, None, (0, 0), to, slot)

    def stage1(unit, e, step):
        if step == 0:
            arrive(unit, None, 0, -e)
            send(unit, 0, (0, -e), (0, e), 4)
            send(unit, 0, (0, -e), (1, 0), 5)
            send(unit, 0, (0, -e), (-1, 0), 6)
        elif step == 1:
            arrive(unit, None, e, 0)
            send(unit, 1, (e, 0), (-e, 0), 7)
            send(unit, 1, (e, 0), (0, 1), 8)
            send(unit, 1, (e, 0), (0, -1), 9)
        elif step == 2:
            arrive(unit, None, 0, e)
            send(unit, 0, (0, e), (1, 0), 10)
            send(unit, 0, (0, e), (-1, 0), 11)
            send(unit, 1, (0, e), (0, -e), 12)
        else:
            arrive(unit, None, -e, 0)
            send(unit, 1, (-e, 0), (0, 1), 13)
            send(unit, 1, (-e, 0), (0, -1), 14)
            send(unit, 0, (-e, 0), (e, 0), 15)

    def stage2(unit, e, step):
        if step == 0:
            arrive(unit, 0, 0, 2)
            send(unit, 0, (0, 2), (1, 0), 16)
            send(unit, 0, (0, 2), (-1, 0), 17)
            arrive(unit, 1, 2, 0)
            send(unit, 1, (2, 0), (0, 1), 18)
            send(unit, 1, (2, 0), (0, -1), 19)
        elif step == 1:
            arrive(unit, 0, -e, 1)
            send(unit, 0, (-e, 1), (e, 0), 20)
            arrive(unit, 1, 1, e)
            send(unit, 1, (1, e), (0, -e), 21)
        else:
            arrive(unit, 0, -e, -1)
            send(unit, 0, (-e, -1), (e, 0), 22)
            arrive(unit, 1, -1, e)
            send(unit, 1, (-1, e), (0, -e), 23)

    def stage3(unit, e):
        arrive(unit, 0, -e, 2)
        send(unit, 0, (-e, 2), (e, 0), 24)
        arrive(unit, 1, 2, e)
        send(unit, 1, (2, e), (0, -e), 25)

    def final(unit):
        def rest(e):
            for ry, rx in ((e, 1), (e, -1), (2, 0), (e, 2), (2, 1), (2, -1), (2, 2)):
                arrive(unit, 0, ry, rx)
            for ry, rx in ((1, -e), (-1, -e), (0, 2), (2, -e), (1, 2), (-1, 2), (2, 2)):
                arrive(unit, 1, ry, rx)

        even = lax.rem(unit, 2) == 0
        pl.when(even)(lambda: rest(1))
        pl.when(jnp.logical_not(even))(lambda: rest(-1))

    def drain_shares(count):
        def body(unit, _):
            for slot in range(26):
                ref = tile_part(unit, None if slot < 4 else 0, 0, 0)
                pltpu.make_async_remote_copy(
                    src_ref=ref, dst_ref=ref,
                    send_sem=l_send.at[unit, slot], recv_sem=l_recv.at[unit, 0, 0],
                    device_id=at_plane(0, 1), device_id_type=MESH,
                ).wait_send()
            return 0

        lax.fori_loop(0, count, body, 0)


    def strip(k, which, p):
        start = pl.multiple_of(which * half_panel + p * piece, piece)
        return solved.at[k, pl.ds(start, piece), :]

    def hop(k, which, p, send_sem, recv_sem, to):
        ref = strip(k, which, p)
        return pltpu.make_async_remote_copy(
            src_ref=ref, dst_ref=ref, send_sem=send_sem.at[k, p], recv_sem=recv_sem.at[k, p],
            device_id=(to, col), device_id_type=MESH,
        )

    def relay(j, to_sibling):
        k, p = lax.div(j, PIECES), lax.rem(j, PIECES)
        hop(k, core, p, c_send, c_recv, up).wait_recv()

        @pl.when(hops < 7)
        def _():
            hop(k, core, p, c_send, c_recv, down).start()

        if to_sibling:

            @pl.when(lax.rem(p, GROUP) == GROUP - 1)
            def _():
                beside(k, core, lax.div(p, GROUP)).start()

    def beside(k, which, g):
        rows = GROUP * piece
        ref = solved.at[k, pl.ds(pl.multiple_of(which * half_panel + g * rows, rows), rows), :]
        return pltpu.make_async_remote_copy(
            src_ref=ref, dst_ref=ref, send_sem=b_send.at[k, g], recv_sem=b_recv.at[k, g],
            device_id=(sibling, col), device_id_type=MESH,
        )

    def from_sibling(k):
        for g in range(PIECES // GROUP):
            beside(k, 1 - core, g).wait_recv()


    def convert(src):
        def body(b, _):
            start = pl.multiple_of(b * 32, 32)
            high, low = split(src[pl.ds(start, 32), :])
            right3[pl.ds(start, 32), :] = high
            right3[pl.ds(pl.multiple_of(panel + start, 32), 32), :] = low
            right3[pl.ds(pl.multiple_of(2 * panel + start, 32), 32), :] = high
            return 0

        lax.fori_loop(0, panel // 32, body, 0)

    def unfold(unit):
        def body(b, _):
            start = pl.multiple_of(b * 128, 128)
            for g in range(panel // 128):
                tile = share[unit, pl.ds(start, 128), g * 128 : (g + 1) * 128].T
                high, low = split(tile)
                to = pl.ds(g * 128, 128)
                left3[to, pl.ds(start, 128)] = high
                left3[to, pl.ds(pl.multiple_of(panel + start, 128), 128)] = high
                left3[to, pl.ds(pl.multiple_of(2 * panel + start, 128), 128)] = low
            return 0

        lax.fori_loop(0, panel // 128, body, 0)

    def product(block, dest):
        cols = pl.ds(pl.multiple_of(block * 256, 256), 256)
        to = pl.ds(pl.multiple_of(dest * panel, panel), panel)
        acc = jnp.dot(left3[...], right3[:, cols], preferred_element_type=F32)
        return cols, to, acc

    def subtract(block, dest):
        cols, to, acc = product(block, dest)
        out[to, cols] = out[to, cols] - acc

    def assign(block, dest, k):
        cols, to, acc = product(block, dest)
        out[to, cols] = acc
        solved[k, :, cols] = acc


    half3 = 3 * half_panel

    def convert_half(k, which, turn):
        def body(b, _):
            start = pl.multiple_of(b * 32, 32)
            high, low = split(solved[k, pl.ds(pl.multiple_of(which * half_panel + start, 32), 32), :])
            for i, v in enumerate((high, low, high)):
                right3[pl.ds(pl.multiple_of(turn * half3 + i * half_panel + start, 32), 32), :] = v
            return 0

        lax.fori_loop(0, half_panel // 32, body, 0)

    def unfold_half(unit, which):
        for b in range(half_panel // 128):
            start = pl.multiple_of(which * half_panel + b * 128, 128)
            for g in range(panel // 128):
                high, low = split(share[unit, pl.ds(start, 128), g * 128 : (g + 1) * 128].T)
                for i, v in enumerate((high, high, low)):
                    left3[g * 128 : (g + 1) * 128, i * half_panel + b * 128 : i * half_panel + (b + 1) * 128] = v

    def subtract_half(block, dest, turn):
        cols = pl.ds(block * 256, 256)
        to = pl.ds(pl.multiple_of(dest * panel, panel), panel)
        acc = jnp.dot(left3[:, :half3], right3[turn * half3 : (turn + 1) * half3, cols], preferred_element_type=F32)
        out[to, cols] = out[to, cols] - acc

    def subtract_ahead(k):
        def body(block, _):
            cols, _, acc = product(block, 0)
            solved[k, :, cols] = solved[k, :, cols] - acc
            return 0

        lax.fori_loop(0, 3, body, 0)

    def assign_ahead(k):
        def body(block, _):
            cols, _, acc = product(block, 0)
            solved[k, :, cols] = acc
            return 0

        lax.fori_loop(0, 3, body, 0)

    def subtract_all(dest):
        def body(block, _):
            subtract(block, dest)
            return 0

        lax.fori_loop(0, 3, body, 0)

    def assign_all(dest, k):
        def body(block, _):
            assign(block, dest, k)
            return 0

        lax.fori_loop(0, 3, body, 0)

    def out_panel(u):
        return out.at[pl.ds(pl.multiple_of(u * panel, panel), panel), :]


    first, second = row == 0, row == 1

    def loop(first, last, body):
        def turn(i, _):
            body(i)
            return 0

        lax.fori_loop(first, last, turn, 0)

    fetch = pltpu.make_async_copy(rhs, out, io_sem.at[0])
    fetch.start()

    def mine(t):
        return share.at[t, pl.ds(pl.multiple_of(col * slab, slab), slab), :]

    def take_factor(t, k, u):
        columns = pl.ds(pl.multiple_of(u * panel, panel), panel)
        return pltpu.make_async_copy(pan.at[k, :, columns], mine(t), take_sem.at[t])

    def take_inverse(t, k):
        return pltpu.make_async_copy(diag.at[k], mine(t), take_sem.at[t])

    @pl.when(row > 1)
    def _():
        loop(0, UNITS, lambda t: take_factor(t, t // 3, t % 3).start())

    @pl.when(first)
    def _():
        take_inverse(0, 0).start()
        take_factor(1, 0, 1).start()
        take_inverse(2, 1).start()

    @pl.when(second)
    def _():
        take_factor(0, 0, 0).start()
        take_inverse(3, 2).start()
        take_factor(4, 1, 0).start()
        take_factor(5, 2, 0).start()
        take_inverse(6, 3).start()
        loop(0, 8, lambda j: take_factor(EARLY + j, lax.div(j, 2), 1 + lax.rem(j, 2)).start())

    def handed(i):
        columns = pl.ds(2 * panel, panel)
        src, dst = (
            (rhs.at[columns, :], solved.at[2]),
            (pan.at[0, :, columns], mine(1)),
            (pan.at[1, :, columns], mine(2)),
            (solved.at[2], solved.at[2]),
        )[i]
        return pltpu.make_async_remote_copy(
            src_ref=src, dst_ref=dst, send_sem=h_send.at[i], recv_sem=h_recv.at[i],
            device_id=(sibling, col), device_id_type=MESH,
        )

    barrier = pltpu.get_barrier_semaphore()
    for to in (at_plane(0, 1), at_plane(0, -1), at_plane(1, 0), at_plane(-1, 0), (sibling, col), (up, col), (down, col)):
        pl.semaphore_signal(barrier, inc=1, device_id=to, device_id_type=MESH)

    for pair in ((1, 2), (2, 1)):

        @pl.when(row == pair[0])
        def _():
            pl.semaphore_signal(barrier, inc=1, device_id=(pair[1], col), device_id_type=MESH)

    loop(0, jnp.where(first, HEAD, jnp.where(second, 1, UNITS)), lambda t: take_inverse(t, 0).wait())

    @pl.when(second)
    def _():
        loop(3, SLOTS, lambda t: take_inverse(t, 0).wait())

    pl.semaphore_wait(barrier, jnp.where((row == 1) | (row == 2), 8, 7))


    def plane_turn(m, first_unit, last_unit):
        @pl.when(m + 2 < last_unit)
        def _():
            stage0(m + 2)

        def relays(e):
            @pl.when(m < last_unit)
            def _():
                for i in range(4):
                    stage1(m, e, i)

            @pl.when((m >= first_unit + 1) & (m < last_unit + 1))
            def _():
                for i in range(3):
                    stage2(m - 1, -e, i)

            @pl.when((m >= first_unit + 2) & (m < last_unit + 2))
            def _():
                stage3(m - 2, e)

        even = lax.rem(m, 2) == 0
        pl.when(even)(lambda: relays(1))
        pl.when(jnp.logical_not(even))(lambda: relays(-1))

    @pl.when(first)
    def _():
        for i in (1, 2):
            handed(i).start()
        stage0(0)
        stage0(1)
        handed(0).start()

        def turn(m):
            @pl.when(m == GO)
            def _():
                pl.semaphore_signal(go_sem, inc=1, device_id=(sibling, col), device_id_type=MESH)

            plane_turn(m, 0, HEAD)

            @pl.when(m == 3)
            def _():
                fetch.wait()

            @pl.when(m >= 3)
            def _():
                q = m - 3
                final(q)
                k = jnp.where(q < 2, 0, 1)
                convert(out_panel(k))
                unfold(q)

                @pl.when(q != 1)
                def _():
                    assign_all(k, k)
                    for p in range(PIECES):
                        hop(k, 0, p, c_send, c_recv, down).start()
                        hop(k, 1, p, x_send, c_recv, sibling).start()
                    for g in range(PIECES // GROUP):
                        beside(k, 0, g).start()

                @pl.when(q == 1)
                def _():
                    subtract_all(1)

        loop(0, HEAD + 3, turn)
        handed(3).wait_recv()
        back = pltpu.make_async_copy(solved.at[2], out.at[pl.ds(2 * panel, panel), :], io_sem.at[0])
        back.start()
        drain_shares(HEAD)

        def drain(j):
            k, p = lax.div(j, PIECES), lax.rem(j, PIECES)
            hop(k, 0, p, c_send, c_recv, down).wait_send()
            hop(k, 1, p, x_send, c_recv, sibling).wait_send()

            @pl.when(lax.rem(p, GROUP) == 0)
            def _():
                beside(k, 0, lax.div(p, GROUP)).wait_send()

        loop(0, 2 * PIECES, drain)
        for i in range(3):
            handed(i).wait_send()
        back.wait()

    @pl.when(second)
    def _():
        pl.semaphore_wait(go_sem, 1)
        stage0(0)
        for i in (1, 2):
            handed(i).wait_recv()
        stage0(1)

        def pass_on(k):
            for p in range(PIECES):
                hop(k, 1, p, c_send, c_recv, down).start()
                hop(k, 0, p, x_send, c_recv, 2).start()

        def early_turn(m):
            plane_turn(m, 0, SLOTS)

            @pl.when(m >= 3)
            def _():
                q = m - 3
                final(q)

                @pl.when((q == 0) | (q == 2))
                def _():
                    k = lax.div(q, 2)
                    loop(k * PIECES, (k + 1) * PIECES, lambda j: relay(j, False))
                    from_sibling(k)

                @pl.when(q == 0)
                def _():
                    fetch.wait()

                @pl.when(q == 1)
                def _():
                    handed(0).wait_recv()

                @pl.when(q == 6)
                def _():
                    convert(out_panel(0))

                @pl.when((q != 1) & (q != 6))
                def _():
                    convert(solved.at[jnp.where(q == 0, 0, jnp.where((q == 2) | (q == 4), 1, 2))])

                unfold(q)

                @pl.when((q == 0) | (q == 4) | (q == 5))
                def _():
                    subtract_all(0)

                @pl.when((q == 1) | (q == 2))
                def _():
                    subtract_ahead(2)

                @pl.when(q == 3)
                def _():
                    assign_ahead(2)
                    pass_on(2)
                    handed(3).start()

                @pl.when(q == 6)
                def _():
                    assign_all(0, 3)
                    pass_on(3)

        loop(0, EARLY + 3, early_turn)
        def turn(m):
            plane_turn(m, 0, SLOTS)

            @pl.when(m >= EARLY + 3)
            def _():
                q = m - 3
                j = q - EARLY
                final(q)

                @pl.when(lax.rem(j, 2) == 0)
                def _():
                    convert(solved.at[lax.div(j, 2)])

                unfold(q)
                subtract_all(1 + lax.rem(j, 2))

        loop(EARLY + 3, SLOTS + 3, turn)
        drain_shares(SLOTS)
        loop(0, 4 * PIECES, lambda j: hop(lax.div(j, PIECES), 1, lax.rem(j, PIECES), c_send, c_recv, down).wait_send())
        loop(2 * PIECES, 4 * PIECES, lambda j: hop(lax.div(j, PIECES), 0, lax.rem(j, PIECES), x_send, c_recv, 2).wait_send())
        handed(3).wait_send()


    @pl.when(row > 1)
    def _():
        near = hops <= 4
        halves = (jnp.where(near, core, 1 - core), jnp.where(near, 1 - core, core))
        lags = [
            lax.div(S_FIRST + S_HOP * h + 16 + 3, 4)
            for h in (jnp.minimum(hops, 8 - hops), jnp.maximum(hops, 8 - hops))
        ]
        due = S_FIRST + S_HOP * hops

        def relayed(spot):
            ahead = jnp.maximum(spot - due, 0)
            return jnp.minimum(lax.div(ahead * S_NUM, S_DEN), 4 * PIECES)

        def taken(slot, lag):
            ready = jnp.minimum(slot - lag + 1, lax.div(jnp.maximum(slot - SLACK + 2, 0), 2))
            return jnp.clip(ready, 0, UNITS)

        stage0(0)
        stage0(1)

        def tile_turn(m, e, carry):
            before, done = list(carry[:2]), carry[2]
            for i in range(SPOTS):
                if i == 0:

                    @pl.when(m + 2 < UNITS)
                    def _():
                        stage0(m + 2)

                if i % 2 == 0:

                    @pl.when(m < UNITS)
                    def _():
                        stage1(m, e, i // 2)
                elif i < 7:

                    @pl.when((m >= 2) & (m < UNITS + 2))
                    def _():
                        stage2(m - 2, e, i // 2)
                else:

                    @pl.when((m >= 3) & (m < UNITS + 3))
                    def _():
                        stage3(m - 3, -e)

                now = relayed(m * SPOTS + i)
                loop(done, now, lambda j: relay(j, True))
                done = now

                turn = (i % 4) // 2
                if i % 2 == 0:
                    after = taken(2 * m + i // 4, lags[turn])
                    q = after - 1
                    k, u = lax.div(jnp.maximum(q, 0), 3), lax.rem(jnp.maximum(q, 0), 3)
                    fresh = after > before[turn]
                    before[turn] = after

                    @pl.when(fresh)
                    def _():
                        if turn == 0:
                            final(q)

                            @pl.when(q == 0)
                            def _():
                                fetch.wait()

                        @pl.when(u == 0)
                        def _():
                            pl.when(near if turn == 1 else jnp.logical_not(near))(lambda: from_sibling(k))
                            convert_half(k, halves[turn], turn)

                        unfold_half(q, halves[turn])
                        subtract_half(0, u, turn)
                else:

                    @pl.when(fresh)
                    def _():
                        subtract_half(1, u, turn)
                        subtract_half(2, u, turn)

            return before[0], before[1], done

        def turn(t, carry):
            carry = tile_turn(2 * t, 1, carry)
            return tile_turn(2 * t + 1, -1, carry)

        lax.fori_loop(0, TURNS, turn, (jnp.int32(0),) * 3)
        drain_shares(UNITS)

        def drain(j):
            k, p = j // PIECES, j % PIECES

            @pl.when(hops < 7)
            def _():
                hop(k, core, p, c_send, c_recv, down).wait_send()

            @pl.when(lax.rem(p, GROUP) == 0)
            def _():
                beside(k, core, lax.div(p, GROUP)).wait_send()

        loop(0, 4 * PIECES, drain)


def per_device(rhs, panels_l, diag_inverse):
    rows, width = rhs.shape
    count, panel, _ = diag_inverse.shape
    sem = pltpu.SemaphoreType.DMA
    return pl.pallas_call(
        kernel,
        out_shape=pltpu.VMEM((rows, width), F32),
        in_specs=[pl.BlockSpec(memory_space=pl.ANY)] * 3,
        out_specs=pl.BlockSpec(memory_space=pltpu.VMEM),
        scratch_shapes=[
            pltpu.VMEM((SLOTS, panel, panel), F32),
            pltpu.VMEM((count, panel, width), F32),
            pltpu.VMEM((3 * panel, width), BF16),
            pltpu.VMEM((panel, 3 * panel), BF16),
            pltpu.SemaphoreType.REGULAR,
            sem((1,)),
            sem((SLOTS,)),
            sem((SLOTS, 2, 16)),
            sem((SLOTS, 26)),
            sem((count, PIECES)),
            sem((count, PIECES)),
            sem((count, PIECES // GROUP)),
            sem((count, PIECES // GROUP)),
            sem((count, PIECES)),
            sem((4,)),
            sem((4,)),
        ],
        compiler_params=pltpu.CompilerParams(
            collective_id=0, has_side_effects=True, vmem_limit_bytes=62_200_000
        ),
        name="forward_substitution",
    )(rhs, jnp.swapaxes(panels_l, 1, 2), jnp.swapaxes(diag_inverse, 1, 2))


def solution(mesh):
    in_specs = (P("row", "col"), P(None, "row", "col"), P(None, None, "col"))
    out_specs = P("row", "col")
    return jax.shard_map(
        per_device, mesh=mesh, in_specs=in_specs, out_specs=out_specs, check_vma=False
    )
```
